128 devices in a mesh: heads: 32 (over y, x_lo, z), qgrp: 4 (over x_hi, core).
Axes of the slice: x: 4 (x_hi: 2, x_lo: 2; x = x_hi * 2 + x_lo), y: 4, z: 4, core: 2. Of those that a mesh axis runs over, the one named last changes fastest.
Arguments:
- q_main: bfloat16 [2048, 128, 576], P('qgrp', 'heads'), may hold values from -6 to 6
- latent: bfloat16 [2048, 576], P(('heads', 'qgrp')), may hold values from -6 to 6
- q_index: bfloat16 [2048, 64, 128], P('qgrp', 'heads'), may hold values from -6 to 6
- head_weight: float32 [64, 2048], P('heads', 'qgrp'), may hold values from -1.5 to 1.5
- k_index: bfloat16 [2048, 128], P(('heads', 'qgrp')), may hold values from -6 to 6
- token_weight: float32 [2048], P('qgrp'), may hold values from 4 to 32
- block_order: int32 [8], replicated, may hold values from 0 to 7, each once
Outputs:
- grad_q_index: float32 [2048, 64, 128], P('qgrp', 'heads')
- grad_head_weight: float32 [64, 2048], P('heads', 'qgrp')
- grad_k_index: float32 [2048, 128], P(('heads', 'qgrp'))
The draws below stay inside these ranges and needn't reach their ends.
Inputs may be any that keep to these rules, and one draw needn't show every extreme that they name: `block_order`: a permutation of the half-blocks.
All inputs are finite; a program needn't handle non-finite values.
Results may differ from the reference program's by a relative error of at most 0.0065.
Values may be sent and summed in bfloat16 or wider, within the bound.
A program may use at most 128 MiB of HBM per device.

```python
import math
import jax
import jax.numpy as jnp
from jax import lax

HEADS = 128
LATENT = 576
IHEADS = 64
IDIM = 128
HALF = 256
HALVES = 8
WINDOW = 2048


def drawn_values(key, shape):
    return jnp.clip(jax.random.normal(key, shape, jnp.float32), -6.0, 6.0)


def index_weights(key):
    inner = jax.random.fold_in(key, 61)
    return jnp.clip(0.25 * jax.random.normal(inner, (IHEADS, WINDOW), jnp.float32), -1.5, 1.5)


def draw_q_main(key, part):
    inner = jax.random.fold_in(key, 1)
    values = drawn_values(inner, (WINDOW, HEADS, LATENT))
    return values.astype(jnp.bfloat16)


def draw_latent(key, part):
    inner = jax.random.fold_in(key, 2)
    values = drawn_values(inner, (WINDOW, LATENT))
    return values.astype(jnp.bfloat16)


def draw_q_index(key, part):
    inner = jax.random.fold_in(key, 3)
    values = drawn_values(inner, (WINDOW, IHEADS, IDIM))
    return values.astype(jnp.bfloat16)


def draw_head_weight(key, part):
    return index_weights(key)


def draw_k_index(key, part):
    inner = jax.random.fold_in(key, 4)
    values = drawn_values(inner, (WINDOW, IDIM))
    return values.astype(jnp.bfloat16)


def shard_levels(own_key, extent, pieces, low, top_value):
    gain, own = 1.0, jax.random.fold_in(own_key, 6)
    for axis_at, blocks in pieces:
        steps = jnp.exp(jax.random.uniform(jax.random.fold_in(own, axis_at), (blocks,), jnp.float32, low / len(pieces), top_value / len(pieces)))
        gain = gain * jnp.repeat(steps, extent[axis_at] // blocks).reshape([-1 if axis == axis_at else 1 for axis in range(len(extent))])
    return gain


def setup_inputs(seed: int = 0) -> dict:
    key_list = jax.random.split(jax.random.key(seed), 8)
    q_main = draw_q_main(jax.random.fold_in(key_list[7], 71), 0)
    latent = draw_latent(jax.random.fold_in(key_list[7], 71), 0)
    q_index = draw_q_index(jax.random.fold_in(key_list[7], 71), 0)
    head_weight = draw_head_weight(jax.random.fold_in(key_list[7], 71), 0)
    k_index = draw_k_index(jax.random.fold_in(key_list[7], 71), 0)
    token_weight = jnp.clip(jnp.exp(math.log(32.0) - 2.0794415 * jax.random.uniform(key_list[5], (WINDOW,), jnp.float32) ** shard_levels(key_list[5], (WINDOW,), ((0, 4),), -0.2, 0.2)), 4.0, 32.0)
    block_order = jax.random.permutation(key_list[6], HALVES).astype(jnp.int32)
    return dict(q_main=q_main, latent=latent, q_index=q_index, head_weight=head_weight, k_index=k_index, token_weight=token_weight, block_order=block_order)


scale_main = 192.0 ** -0.5
scale_index = 128.0 ** -0.5


def scores(left, right):
    return lax.dot_general(left, right, (((1,), (1,)), ((), ())), preferred_element_type=jnp.float32)


def masked_softmax(values, visible):
    values = jnp.where(visible, values, -jnp.inf)
    top = jnp.max(values, axis=1, keepdims=True)
    expo = jnp.exp(values - top)
    return expo / jnp.sum(expo, axis=1, keepdims=True)


def reference(q_main, latent, q_index, head_weight, k_index, token_weight, block_order):
    rows = jnp.arange(WINDOW, dtype=jnp.int32)
    position = block_order[rows // HALF] * HALF + rows % HALF
    visible = jnp.arange(WINDOW, dtype=jnp.int32)[None, :] <= position[:, None]

    def main_step(head, total):
        query = lax.dynamic_index_in_dim(q_main, head, 1, False)
        return total + masked_softmax(scores(query, latent) * scale_main, visible)

    target = lax.fori_loop(0, HEADS, main_step, jnp.zeros((WINDOW, WINDOW), jnp.float32)) / HEADS

    def index_step(head, total):
        query = lax.dynamic_index_in_dim(q_index, head, 1, False)
        weight = lax.dynamic_index_in_dim(head_weight, head, 0, False)
        return total + weight[:, None] * jax.nn.relu(scores(query, k_index) * scale_index)

    logits = lax.fori_loop(0, IHEADS, index_step, jnp.zeros((WINDOW, WINDOW), jnp.float32))
    probs = masked_softmax(logits, visible)
    dlogits = token_weight[:, None] * (probs - target)

    def back_step(grad_keys, head):
        query = lax.dynamic_index_in_dim(q_index, head, 1, False)
        weight = lax.dynamic_index_in_dim(head_weight, head, 0, False)
        raw = scores(query, k_index) * scale_index
        grad_weight = jnp.sum(dlogits * jax.nn.relu(raw), axis=1)
        grad_raw = (dlogits * weight[:, None] * (raw > 0) * scale_index).astype(jnp.bfloat16)
        grad_query = jnp.dot(grad_raw, k_index, preferred_element_type=jnp.float32)
        grad_keys = grad_keys + lax.dot_general(grad_raw, query, (((0,), (0,)), ((), ())), preferred_element_type=jnp.float32)
        return grad_keys, (grad_query, grad_weight)

    grad_k_index, stacked = lax.scan(back_step, jnp.zeros((WINDOW, IDIM), jnp.float32), jnp.arange(IHEADS, dtype=jnp.int32))
    grad_q_index = jnp.transpose(stacked[0], (1, 0, 2))
    return grad_q_index, stacked[1], grad_k_index
```

```python
import functools

import jax
import jax.numpy as jnp
from jax import lax
from jax.experimental import pallas as pl
from jax.experimental.pallas import tpu as pltpu
from jax.sharding import PartitionSpec as P

MESH = pl.DeviceIdType.MESH
SCALE_MAIN = 192.0 ** (-0.5)
SCALE_INDEX = 128.0 ** (-0.5)
NEG = -3.0e38
BLK = 256
F32 = jnp.float32
BF16 = jnp.bfloat16


def coords():
    h = lax.axis_index("heads")
    q = lax.axis_index("qgrp")
    y, xl, z = h // 8, (h // 4) % 2, h % 4
    xh, c = q // 2, q % 2
    return y, xh * 2 + xl, z, c


def device(y, x, z, c):
    return {"heads": y * 8 + (x % 2) * 4 + z, "qgrp": (x // 2) * 2 + c}


def exchange_kernel(send, wsend, mykeys, recv, wrecv, keys, qs, qr, ws, wr, ls, ags, agr):
    y, x, z, c = coords()
    xl, xh = x % 2, x // 2
    heads, group = y * 8 + xl * 4 + z, xh * 2 + c

    def ag_axis(phase, axis):
        copies = []
        for j in range(1, 4 if axis != "c" else 2):
            if axis == "z":
                ref = keys.at[y, xl, z, xh, c]
                dev = device(y, x, (z + j) % 4, c)
            elif axis == "y":
                ref = keys.at[y, xl, :, xh, c]
                dev = device((y + j) % 4, x, z, c)
            elif axis == "x":
                ref = keys.at[:, xl, :, xh, c]
                dev = device(y, (x + j) % 4, z, c)
            else:
                ref = keys.at[:, :, :, :, c]
                dev = device(y, x, z, 1 - c)
            copies.append(
                pltpu.make_async_remote_copy(
                    src_ref=ref,
                    dst_ref=ref,
                    send_sem=ags.at[phase, j - 1],
                    recv_sem=agr.at[phase, j - 1],
                    device_id=dev,
                    device_id_type=MESH,
                )
            )
        return copies

    def q_send(k, carry):
        dc = k % 2
        dz = (k // 2) % 4
        dy = (k // 8) % 4
        dx = k // 32
        y2, x2, z2, c2 = (y + dy) % 4, (x + dx) % 4, (z + dz) % 4, (c + dc) % 2
        e2 = (y2 * 8 + (x2 % 2) * 4 + z2) * 2 + x2 // 2
        hl = (c2 + c) % 2
        dev = device(y2, x2, z2, c2)
        pltpu.make_async_remote_copy(
            src_ref=send.at[hl * 64 + e2],
            dst_ref=recv.at[group, heads],
            send_sem=qs,
            recv_sem=qr.at[group],
            device_id=dev,
            device_id_type=MESH,
        ).start()
        pltpu.make_async_remote_copy(
            src_ref=wsend.at[hl * 64 + e2],
            dst_ref=wrecv.at[group, heads],
            send_sem=ws,
            recv_sem=wr,
            device_id=dev,
            device_id_type=MESH,
        ).start()
        return carry

    e = heads * 2 + xh
    own = pltpu.make_async_copy(mykeys, keys.at[y, xl, z, xh, c], ls)
    own.start()
    pltpu.make_async_copy(send.at[e], recv.at[group, heads], qr.at[group]).start()
    pltpu.make_async_copy(wsend.at[e], wrecv.at[group, heads], wr).start()
    own.wait()
    phase = ag_axis(0, "z")
    for cp in phase:
        cp.start()
    lax.fori_loop(1, 16, q_send, 0)
    for cp in phase:
        cp.wait()
    phase = ag_axis(1, "y")
    for cp in phase:
        cp.start()
    lax.fori_loop(16, 48, q_send, 0)
    for cp in phase:
        cp.wait()
    phase = ag_axis(2, "x")
    for cp in phase:
        cp.start()
    lax.fori_loop(48, 128, q_send, 0)
    for cp in phase:
        cp.wait()
    phase = ag_axis(3, "c")
    for cp in phase:
        cp.start()
    for cp in phase:
        cp.wait()
    for g in range(4):
        pltpu.make_async_copy(recv.at[g], recv.at[g], qr.at[g]).wait()
    pltpu.make_async_copy(wrecv, wrecv, wr).wait()
    pltpu.make_async_copy(send.at[pl.ds(0, 127)], send.at[pl.ds(0, 127)], qs).wait()
    pltpu.make_async_copy(wsend.at[pl.ds(0, 127)], wsend.at[pl.ds(0, 127)], ws).wait()


def exchange(send, wsend, mykeys):
    any_spec = pl.BlockSpec(memory_space=pl.ANY)
    return pl.pallas_call(
        exchange_kernel,
        out_shape=(
            jax.ShapeDtypeStruct((4, 32, 16, 640), BF16),
            jax.ShapeDtypeStruct((4, 32, 1, 128), F32),
            jax.ShapeDtypeStruct((4, 2, 4, 2, 2, 16, 768), BF16),
        ),
        in_specs=[any_spec] * 3,
        out_specs=(any_spec,) * 3,
        scratch_shapes=[
            pltpu.SemaphoreType.DMA,
            pltpu.SemaphoreType.DMA((4,)),
            pltpu.SemaphoreType.DMA,
            pltpu.SemaphoreType.DMA,
            pltpu.SemaphoreType.DMA,
            pltpu.SemaphoreType.DMA((4, 3)),
            pltpu.SemaphoreType.DMA((4, 3)),
        ],
        compiler_params=pltpu.CompilerParams(has_side_effects=True),
        name="exchange",
    )(send, wsend, mykeys)


def dot_t(a, b):
    return lax.dot_general(a, b, (((1,), (1,)), ((), ())), preferred_element_type=F32)


def compute_kernel(meta, recv, wrecv, keys, gq, gw, gk, s_buf, r_buf, gkt, l8, t16, m_buf, d_buf, gq_acc, gw_acc):
    g = pl.program_id(0)
    b = meta[g]
    e = meta[4]
    nb = b + 1

    @pl.when(g == 0)
    def _():
        gkt[...] = jnp.zeros_like(gkt)

    m_buf[...] = jnp.full_like(m_buf, NEG)

    def main_scores(kb, carry):
        cols = pl.ds(pl.multiple_of(kb * BLK, BLK), BLK)
        x = recv[0].reshape(512, 640)
        s = dot_t(x, keys[cols, 0:640]) * SCALE_MAIN
        row = (lax.broadcasted_iota(jnp.int32, (512, BLK), 0) % 16) // 4
        lane = lax.broadcasted_iota(jnp.int32, (512, BLK), 1)
        s = jnp.where(lane - row <= (b - kb) * BLK + 4 * e, s, NEG)
        s_buf[:, cols] = s
        m_buf[...] = jnp.maximum(m_buf[...], jnp.maximum(s[:, 0:128], s[:, 128:256]))
        return carry

    lax.fori_loop(0, nb, main_scores, 0)
    m_buf[...] = jnp.broadcast_to(jnp.max(m_buf[...], axis=1, keepdims=True), (512, 128))
    d_buf[...] = jnp.zeros_like(d_buf)

    def main_exp(kb, carry):
        cols = pl.ds(pl.multiple_of(kb * BLK, BLK), BLK)
        m = m_buf[...]
        p = jnp.exp(s_buf[:, cols] - jnp.concatenate([m, m], axis=1))
        s_buf[:, cols] = p
        d_buf[...] += p[:, 0:128] + p[:, 128:256]
        return carry

    lax.fori_loop(0, nb, main_exp, 0)
    d_buf[...] = jnp.broadcast_to((1.0 / 128.0) / jnp.sum(d_buf[...], axis=1, keepdims=True), (512, 128))
    t16[...] = jnp.zeros_like(t16)
    l8[...] = jnp.full_like(l8, NEG)

    packed = recv[0, :, :, 512:640].astype(F32)
    low = pltpu.roll(packed[:, 0:8, :].reshape(256, 128), 64, 1)
    lane128 = lax.broadcasted_iota(jnp.int32, (256, 128), 1)
    queries = jnp.where(lane128 < 64, low, packed[:, 8:16, :].reshape(256, 128)).astype(BF16)
    sub = lax.broadcasted_iota(jnp.int32, (32, 8, 128), 1)
    lane3 = lax.broadcasted_iota(jnp.int32, (32, 8, 128), 2)
    wall = jnp.broadcast_to(wrecv[0], (32, 8, 128))
    wcol = jnp.sum(jnp.where(lane3 == sub, wall, 0.0), axis=2, keepdims=True).reshape(256, 1)
    tw8 = jnp.sum(
        jnp.where(lane3[0] == 8 + sub[0] // 2, wall[0], 0.0), axis=1, keepdims=True
    )

    def reduce_and_logits(kb, carry):
        cols = pl.ds(pl.multiple_of(kb * BLK, BLK), BLK)
        d = d_buf[...]
        p = s_buf[:, cols] * jnp.concatenate([d, d], axis=1)
        t16[:, cols] = jnp.sum(p.reshape(32, 16, BLK), axis=0)
        raw = dot_t(queries, keys[cols, 640:768]) * SCALE_INDEX
        relu = jnp.maximum(raw, 0.0)
        r_buf[:, cols] = relu
        l8[:, cols] = jnp.sum((relu * wcol).reshape(32, 8, BLK), axis=0)
        return carry

    lax.fori_loop(0, nb, reduce_and_logits, 0)

    fold_r = lax.broadcasted_iota(jnp.int32, (8, 16), 0)
    fold_c = lax.broadcasted_iota(jnp.int32, (8, 16), 1)
    fold16 = (fold_r // 2 == fold_c // 4).astype(F32)
    fold8 = (fold_r[:, 0:8] // 2 == fold_c[:, 0:8] // 2).astype(F32)
    target = jnp.dot(fold16, t16[...], precision=lax.Precision.HIGHEST, preferred_element_type=F32)
    lane_all = lax.broadcasted_iota(jnp.int32, (8, 2048), 1)
    row_all = lax.broadcasted_iota(jnp.int32, (8, 2048), 0) // 2
    visible = lane_all - row_all <= b * BLK + 4 * e
    lraw = jnp.where(visible, l8[...], 0.0)
    logits = jnp.dot(fold8, lraw, precision=lax.Precision.HIGHEST, preferred_element_type=F32)
    logits = jnp.where(visible, logits, NEG)
    top = jnp.max(logits, axis=1, keepdims=True)
    expo = jnp.where(visible, jnp.exp(logits - top), 0.0)
    probs = expo / jnp.sum(expo, axis=1, keepdims=True)
    l8[...] = tw8 * (probs - target)

    gq_acc[...] = jnp.zeros_like(gq_acc)
    gw_acc[...] = jnp.zeros_like(gw_acc)
    queries_t = queries.T
    wscaled = wcol * SCALE_INDEX

    def backward(kb, carry):
        cols = pl.ds(pl.multiple_of(kb * BLK, BLK), BLK)
        relu = r_buf[:, cols]
        dl = jnp.broadcast_to(l8[:, cols][None], (32, 8, BLK)).reshape(256, BLK)
        gwp = dl * relu
        gw_acc[...] += gwp[:, 0:128] + gwp[:, 128:256]
        grad = jnp.where(relu > 0.0, dl * wscaled, 0.0).astype(BF16)
        gq_acc[...] += jnp.dot(grad, keys[cols, 640:768], preferred_element_type=F32)
        gkt[:, cols] += jnp.dot(queries_t, grad, preferred_element_type=F32)
        return carry

    lax.fori_loop(0, nb, backward, 0)
    gq[0] = gq_acc[...].reshape(32, 8, 128)
    gws = jnp.sum(gw_acc[...], axis=1, keepdims=True).reshape(32, 8, 1)
    gw[0] = jnp.sum(jnp.where(lane3 == sub, gws, 0.0), axis=1, keepdims=True)

    @pl.when(g == 3)
    def _():
        gk[...] = gkt[...].T


def compute(meta, recv, wrecv, keys):
    return pl.pallas_call(
        compute_kernel,
        grid_spec=pltpu.PrefetchScalarGridSpec(
            num_scalar_prefetch=1,
            grid=(4,),
            in_specs=[
                pl.BlockSpec((1, 32, 16, 640), lambda g, meta: (g, 0, 0, 0)),
                pl.BlockSpec((1, 32, 1, 128), lambda g, meta: (g, 0, 0, 0)),
                pl.BlockSpec((2048, 768), lambda g, meta: (0, 0)),
            ],
            out_specs=(
                pl.BlockSpec((1, 32, 8, 128), lambda g, meta: (g, 0, 0, 0)),
                pl.BlockSpec((1, 32, 1, 128), lambda g, meta: (g, 0, 0, 0)),
                pl.BlockSpec((2048, 128), lambda g, meta: (0, 0)),
            ),
            scratch_shapes=[
                pltpu.VMEM((512, 2048), F32),
                pltpu.VMEM((256, 2048), F32),
                pltpu.VMEM((128, 2048), F32),
                pltpu.VMEM((8, 2048), F32),
                pltpu.VMEM((16, 2048), F32),
                pltpu.VMEM((512, 128), F32),
                pltpu.VMEM((512, 128), F32),
                pltpu.VMEM((256, 128), F32),
                pltpu.VMEM((256, 128), F32),
            ],
        ),
        out_shape=(
            jax.ShapeDtypeStruct((4, 32, 8, 128), F32),
            jax.ShapeDtypeStruct((4, 32, 1, 128), F32),
            jax.ShapeDtypeStruct((2048, 128), F32),
        ),
        compiler_params=pltpu.CompilerParams(vmem_limit_bytes=50 * 1024 * 1024),
        name="compute",
    )(meta, recv, wrecv, keys)


def return_kernel(
    gq, gw, gk, gq_out, gw_out, gk_out, rc, v1, rx, v2, ry, v3, rz, qs, qr, ws, wr, rss, rsr
):
    y, x, z, c = coords()
    xl, xh = x % 2, x // 2
    heads, group = y * 8 + xl * 4 + z, xh * 2 + c
    e = heads * 2 + xh

    def remote(phase, j, src, dst, dev):
        return pltpu.make_async_remote_copy(
            src_ref=src,
            dst_ref=dst,
            send_sem=rss.at[phase, j],
            recv_sem=rsr.at[phase, j],
            device_id=dev,
            device_id_type=MESH,
        )

    core = remote(0, 0, gk.at[:, :, :, :, 1 - c], rc, device(y, x, z, 1 - c))
    core.start()

    def q_send(k, carry):
        dc = k % 2
        dz = (k // 2) % 4
        dy = (k // 8) % 4
        dx = k // 32
        y2, x2, z2, c2 = (y + dy) % 4, (x + dx) % 4, (z + dz) % 4, (c + dc) % 2
        heads2, group2 = y2 * 8 + (x2 % 2) * 4 + z2, (x2 // 2) * 2 + c2
        slot = ((c2 + c) % 2) * 64 + e
        dev = device(y2, x2, z2, c2)
        pltpu.make_async_remote_copy(
            src_ref=gq.at[group2, heads2],
            dst_ref=gq_out.at[slot],
            send_sem=qs,
            recv_sem=qr,
            device_id=dev,
            device_id_type=MESH,
        ).start()
        pltpu.make_async_remote_copy(
            src_ref=gw.at[group2, heads2],
            dst_ref=gw_out.at[slot],
            send_sem=ws,
            recv_sem=wr,
            device_id=dev,
            device_id_type=MESH,
        ).start()
        return carry

    pltpu.make_async_copy(gq.at[group, heads], gq_out.at[e], qr).start()
    pltpu.make_async_copy(gw.at[group, heads], gw_out.at[e], wr).start()
    lax.fori_loop(1, 48, q_send, 0)
    core.wait()
    v1[...] = gk[:, :, :, :, c] + rc[...]
    phase = []
    for j in range(1, 4):
        x2 = (x + j) % 4
        phase.append(
            remote(1, j - 1, v1.at[:, x2 % 2, :, x2 // 2], rx.at[j - 1], device(y, x2, z, c))
        )
    for cp in phase:
        cp.start()
    lax.fori_loop(48, 88, q_send, 0)
    for cp in phase:
        cp.wait()
    v2[...] = v1[:, xl, :, xh] + rx[0] + rx[1] + rx[2]
    phase = []
    for j in range(1, 4):
        y2 = (y + j) % 4
        phase.append(remote(2, j - 1, v2.at[y2], ry.at[j - 1], device(y2, x, z, c)))
    for cp in phase:
        cp.start()
    lax.fori_loop(88, 128, q_send, 0)
    for cp in phase:
        cp.wait()
    v3[...] = v2[y] + ry[0] + ry[1] + ry[2]
    phase = []
    for j in range(1, 4):
        z2 = (z + j) % 4
        phase.append(remote(3, j - 1, v3.at[z2], rz.at[j - 1], device(y, x, z2, c)))
    for cp in phase:
        cp.start()
    for cp in phase:
        cp.wait()
    gk_out[...] = v3[z] + rz[0] + rz[1] + rz[2]
    pltpu.make_async_copy(gq_out, gq_out, qr).wait()
    pltpu.make_async_copy(gw_out, gw_out, wr).wait()
    flat = gq_out.at[pl.ds(0, 127)]
    pltpu.make_async_copy(flat, flat, qs).wait()
    flat = gw_out.at[pl.ds(0, 127)]
    pltpu.make_async_copy(flat, flat, ws).wait()


def send_back(gq, gw, gk):
    any_spec = pl.BlockSpec(memory_space=pl.ANY)
    vmem = pl.BlockSpec(memory_space=pltpu.VMEM)
    return pl.pallas_call(
        return_kernel,
        out_shape=(
            jax.ShapeDtypeStruct((128, 8, 128), F32),
            jax.ShapeDtypeStruct((128, 1, 128), F32),
            jax.ShapeDtypeStruct((16, 128), F32),
        ),
        in_specs=[any_spec, any_spec, vmem],
        out_specs=(any_spec, any_spec, vmem),
        scratch_shapes=[
            pltpu.VMEM((4, 2, 4, 2, 16, 128), F32),
            pltpu.VMEM((4, 2, 4, 2, 16, 128), F32),
            pltpu.VMEM((3, 4, 4, 16, 128), F32),
            pltpu.VMEM((4, 4, 16, 128), F32),
            pltpu.VMEM((3, 4, 16, 128), F32),
            pltpu.VMEM((4, 16, 128), F32),
            pltpu.VMEM((3, 16, 128), F32),
            pltpu.SemaphoreType.DMA,
            pltpu.SemaphoreType.DMA,
            pltpu.SemaphoreType.DMA,
            pltpu.SemaphoreType.DMA,
            pltpu.SemaphoreType.DMA((4, 3)),
            pltpu.SemaphoreType.DMA((4, 3)),
        ],
        compiler_params=pltpu.CompilerParams(has_side_effects=True),
        name="send_back",
    )(gq, gw, gk)


def on_device(q_main, latent, q_index, head_weight, k_index, token_weight, block_order):
    packed_index = q_index.reshape(128, 8, 2, 64).transpose(0, 2, 1, 3).reshape(128, 16, 64)
    send = jnp.concatenate([q_main.reshape(128, 16, 576), packed_index], axis=2)
    weights = head_weight.reshape(2, 128, 4).transpose(1, 2, 0).reshape(128, 8)
    wsend = jnp.concatenate(
        [weights, token_weight.reshape(128, 4), jnp.zeros((128, 116), F32)], axis=1
    ).reshape(128, 1, 128)
    mykeys = jnp.concatenate([latent, jnp.zeros((16, 64), BF16), k_index], axis=1)
    recv, wrecv, keys = exchange(send, wsend, mykeys)
    h = lax.axis_index("heads")
    q = lax.axis_index("qgrp")
    core = q % 2
    halves = jnp.stack([2 * g + (core + g) % 2 for g in range(4)])
    meta = jnp.concatenate([block_order[halves], jnp.stack([h * 2 + q // 2])]).astype(jnp.int32)
    gq, gw, gk = compute(meta, recv, wrecv, keys.reshape(2048, 768))
    gq_out, gw_out, gk_out = send_back(gq, gw, gk.reshape(4, 2, 4, 2, 2, 16, 128))
    grad_q = gq_out.reshape(512, 2, 128)
    grad_w = gw_out[:, 0, 0:8].reshape(512, 2).T
    return grad_q, grad_w, gk_out


def solution(mesh):
    return jax.shard_map(
        on_device,
        mesh=mesh,
        in_specs=(
            P("qgrp", "heads", None),
            P(("heads", "qgrp"), None),
            P("qgrp", "heads", None),
            P("heads", "qgrp"),
            P(("heads", "qgrp"), None),
            P("qgrp"),
            P(),
        ),
        out_specs=(P("qgrp", "heads", None), P("heads", "qgrp"), P(("heads", "qgrp"), None)),
        check_vma=False,
    )
```

```python
import math
import random

import jax
import jax.numpy as jnp
from jax import lax
from jax.experimental import pallas as pl
from jax.experimental.pallas import tpu as pltpu
from jax.sharding import PartitionSpec as P

MESH = pl.DeviceIdType.MESH
SCALE_INDEX = 128.0 ** (-0.5)
EXP_SCALE = 192.0 ** (-0.5) * math.log2(math.e)
NEG = -3.0e38
BLK = 256
F32 = jnp.float32
BF16 = jnp.bfloat16
HIGHEST = lax.Precision.HIGHEST


def far_first():
    every = [(a, b, c, d) for a in range(4) for b in range(4) for c in range(4) for d in range(2)][1:]
    random.Random(1).shuffle(every)
    return sorted(every, key=lambda o: sum(min(v, 4 - v) for v in o[:3]) + o[3] * 0.5)[::-1]


ORDER = far_first()
KEY_CUTS = (0, 16, 40, 80, 127)


class Place:
    def __init__(self):
        h = lax.axis_index("heads")
        q = lax.axis_index("qgrp")
        self.y = [lax.rem(lax.div(h, 8) + k, 4) for k in range(4)]
        self.z = [lax.rem(lax.rem(h, 4) + k, 4) for k in range(4)]
        x = lax.div(q, 2) * 2 + lax.rem(lax.div(h, 4), 2)
        self.x = [lax.rem(x + k, 4) for k in range(4)]
        self.c = [lax.rem(q, 2), 1 - lax.rem(q, 2)]
        self.x_low = [lax.rem(v, 2) for v in self.x]
        self.x_high = [lax.div(v, 2) for v in self.x]
        self.y8 = [v * 8 for v in self.y]
        self.xl4 = [v * 4 for v in self.x_low]
        self.xh2 = [v * 2 for v in self.x_high]
        self.heads, self.group = self.at((0, 0, 0, 0))
        self.flat = self.heads * 4 + self.group

    def at(self, o):
        dx, dy, dz, dc = o
        return self.y8[dy] + self.xl4[dx] + self.z[dz], self.xh2[dx] + self.c[dc]


def dev(heads, group):
    return {"heads": heads, "qgrp": group}


def enter(place):
    sem = pltpu.get_barrier_semaphore()
    for o in ORDER:
        pl.semaphore_signal(sem, inc=1, device_id=dev(*place.at(o)), device_id_type=MESH)
    return sem


def exchange_kernel(packed, wsend, mykeys, recv, wrecv, keys, qs, qr, ws, wr, ls, ags, agr):
    p = Place()
    barrier = enter(p)
    mine = pl.ds(p.group * 2, 2)

    def key_phase(number):
        copies = []
        for color, axes in enumerate(("zyx", "yxz", "xzy")):
            lanes = pl.ds(color * 256, 256)
            done = axes[:number]
            at = (
                slice(None) if "y" in done else p.y[0],
                slice(None) if "x" in done else p.x_low[0],
                slice(None) if "z" in done else p.z[0],
                slice(None) if "x" in done else p.x_high[0],
                p.c[0],
                slice(None),
                lanes,
            )
            ref = keys.at[at]
            for j in range(1, 4):
                o = tuple(j if axis == axes[number] else 0 for axis in "xyz") + (0,)
                copies.append(
                    pltpu.make_async_remote_copy(
                        src_ref=ref,
                        dst_ref=ref,
                        send_sem=ags.at[number, color * 3 + j - 1],
                        recv_sem=agr.at[number, color * 3 + j - 1],
                        device_id=dev(*p.at(o)),
                        device_id_type=MESH,
                    )
                )
        return copies

    def core_phase():
        ref = keys.at[:, :, :, :, p.c[0]]
        return [
            pltpu.make_async_remote_copy(
                src_ref=ref,
                dst_ref=ref,
                send_sem=ags.at[3, 0],
                recv_sem=agr.at[3, 0],
                device_id=dev(*p.at((0, 0, 0, 1))),
                device_id_type=MESH,
            )
        ]

    def send(o):
        heads, group = p.at(o)
        e = heads * 4 + group
        for source, target, ssem, rsem in (
            (packed.at[:, e], recv.at[mine, p.heads], qs, qr),
            (wsend.at[e], wrecv.at[p.group, p.heads], ws, wr),
        ):
            pltpu.make_async_remote_copy(
                src_ref=source,
                dst_ref=target,
                send_sem=ssem,
                recv_sem=rsem,
                device_id=dev(heads, group),
                device_id_type=MESH,
            ).start()

    own = pltpu.make_async_copy(mykeys, keys.at[p.y[0], p.x_low[0], p.z[0], p.x_high[0], p.c[0]], ls)
    own.start()
    pltpu.make_async_copy(packed.at[:, p.flat], recv.at[mine, p.heads], qr).start()
    pltpu.make_async_copy(wsend.at[p.flat], wrecv.at[p.group, p.heads], wr).start()
    own.wait()
    pl.semaphore_wait(barrier, 127)
    for number in range(4):
        phase = key_phase(number) if number < 3 else core_phase()
        for cp in phase:
            cp.start()
        for o in ORDER[KEY_CUTS[number] : KEY_CUTS[number + 1]]:
            send(o)
        for cp in phase:
            cp.wait()
    for ref, sem in ((recv, qr), (wrecv, wr)):
        pltpu.make_async_copy(ref, ref, sem).wait()
    part = packed.at[:, pl.ds(0, 127)]
    pltpu.make_async_copy(part, part, qs).wait()
    part = wsend.at[pl.ds(0, 127)]
    pltpu.make_async_copy(part, part, ws).wait()


def exchange(packed, wsend, mykeys):
    any_spec = pl.BlockSpec(memory_space=pl.ANY)
    vmem = pl.BlockSpec(memory_space=pltpu.VMEM)
    return pl.pallas_call(
        exchange_kernel,
        out_shape=(
            jax.ShapeDtypeStruct((8, 32, 8, 640), BF16),
            jax.ShapeDtypeStruct((4, 32, 1, 128), F32),
            jax.ShapeDtypeStruct((4, 2, 4, 2, 2, 16, 768), BF16),
        ),
        in_specs=[any_spec] * 3,
        out_specs=(vmem,) * 3,
        scratch_shapes=[pltpu.SemaphoreType.DMA] * 5
        + [pltpu.SemaphoreType.DMA((4, 9)), pltpu.SemaphoreType.DMA((4, 9))],
        compiler_params=pltpu.CompilerParams(has_side_effects=True, collective_id=1),
        name="exchange",
    )(packed, wsend, mykeys)


def iota(shape, dim):
    return lax.broadcasted_iota(jnp.int32, shape, dim)


def dot_t(a, b, precision=None):
    return lax.dot_general(
        a, b, (((1,), (1,)), ((), ())), precision=precision, preferred_element_type=F32
    )


def dot(a, b, precision=None):
    return jnp.dot(a, b, precision=precision, preferred_element_type=F32)


def one_hot(mask):
    return jnp.where(mask, 1.0, 0.0)


def pack_kernel(main, index, weight, token, latent, key, packed, wsend, mykeys):
    both = jnp.concatenate([main[h] for h in range(4)], axis=1)
    out, src = iota((512, 512), 0), iota((512, 512), 1)
    perm = one_hot(out == (src % 128) * 4 + src // 128).astype(BF16)
    rows = dot_t(perm, both)
    out, src = iota((512, 256), 0), iota((512, 256), 1)
    pick = one_hot(src == out // 2).astype(BF16)
    tail = dot(pick, index[...].reshape(256, 128))
    lane, row = iota((512, 128), 1), iota((512, 128), 0)
    tail = jnp.where(row % 2 == 0, pltpu.roll(tail, 64, 1), tail)
    last = jnp.concatenate([rows[:, 512:576], jnp.zeros((512, 64), F32)], axis=1)
    last = jnp.where(lane < 64, last, tail)
    full = jnp.concatenate([rows[:, 0:512], last], axis=1).astype(BF16)
    packed[0] = full.reshape(64, 8, 640)

    @pl.when(pl.program_id(0) == 0)
    def _():
        total = jnp.zeros((128, 128), F32)
        sub = iota((128, 256), 0)
        for hl in range(2):
            cols = slice(hl * 256, hl * 256 + 256)
            for i in range(2):
                table = jnp.zeros((128, 256), F32)
                for at, line in (
                    (hl * 4 + i * 2, weight[0:1, cols]),
                    (hl * 4 + i * 2 + 1, weight[1:2, cols]),
                    (8 + hl * 2 + i, token[0:1, cols]),
                ):
                    table = jnp.where(sub == at, jnp.broadcast_to(line, (128, 256)), table)
                choose = one_hot(iota((128, 256), 1) == iota((128, 256), 0) * 2 + i)
                total = total + dot_t(choose, table, HIGHEST)
        wsend[...] = total.reshape(128, 1, 128)
        mykeys[:, 0:576] = latent[...]
        mykeys[:, 576:640] = jnp.zeros((16, 64), BF16)
        mykeys[:, 640:768] = key[...]


def pack(q_main, q_index, head_weight, token_weight, latent, k_index):
    return pl.pallas_call(
        pack_kernel,
        grid=(4,),
        in_specs=[
            pl.BlockSpec((4, 576, 128), lambda t: (0, 0, t)),
            pl.BlockSpec((256, 128), lambda t: (t, 0)),
            pl.BlockSpec((2, 512), lambda t: (0, 0)),
            pl.BlockSpec((1, 512), lambda t: (0, 0)),
            pl.BlockSpec((16, 576), lambda t: (0, 0)),
            pl.BlockSpec((16, 128), lambda t: (0, 0)),
        ],
        out_specs=(
            pl.BlockSpec((1, 64, 8, 640), lambda t: (t // 2, t % 2, 0, 0)),
            pl.BlockSpec((128, 1, 128), lambda t: (0, 0, 0)),
            pl.BlockSpec((16, 768), lambda t: (0, 0)),
        ),
        out_shape=(
            jax.ShapeDtypeStruct((2, 128, 8, 640), BF16),
            jax.ShapeDtypeStruct((128, 1, 128), F32),
            jax.ShapeDtypeStruct((16, 768), BF16),
        ),
        name="pack",
    )(
        jnp.transpose(q_main, (1, 2, 0)),
        q_index.reshape(1024, 128),
        head_weight,
        token_weight.reshape(1, 512),
        latent,
        k_index,
    )


def compute_kernel(meta, recv, wrecv, keys, gq, gw, gk, s_buf, r_buf, gkt, t_buf, l_buf, wtab, gwtab):
    e2 = meta[8] * 2
    wtab[...] = wrecv[...].reshape(4, 32, 128)
    gwtab[...] = jnp.zeros_like(gwtab)
    v128, l128 = iota((128, 128), 0), iota((128, 128), 1)
    spread = one_hot(iota((128, 32), 1) == iota((128, 32), 0) // 4)
    gather = one_hot(iota((32, 128), 1) // 4 == iota((32, 128), 0))
    even = one_hot(iota((128, 256), 1) == iota((128, 256), 0) * 2).astype(BF16)
    odd = one_hot(iota((128, 256), 1) == iota((128, 256), 0) * 2 + 1).astype(BF16)
    f_out, f_in = iota((8, 8), 0), iota((8, 8), 1)
    fold_t = one_hot(f_in // 4 == (f_out // 2) % 2)
    fold_l = one_hot((f_in // 2) % 2 == (f_out // 2) % 2)

    for b in range(8):
        n = (b + 1) * BLK
        h = meta[b]
        g, hl = lax.div(h, 2), lax.rem(h, 2)
        par = b % 2
        x = recv[h]
        for kb in range(b + 1):
            cols = slice(kb * BLK, kb * BLK + BLK)
            s = dot_t(x, keys[cols, 0:640])
            if kb == b:
                row = (iota((256, BLK), 0) % 8) // 4
                s = jnp.where(iota((256, BLK), 1) - row <= e2, s, NEG)
            s_buf[par, :, cols] = s

        def softmax_rows(r, total):
            rows = pl.ds(pl.multiple_of(r * 32, 32), 32)
            s = s_buf[par, rows, 0:n]
            top = jnp.max(s, axis=1, keepdims=True)
            p = jnp.exp2((s - top) * EXP_SCALE)
            inv = (1.0 / 128.0) / jnp.sum(p, axis=1, keepdims=True)
            t_buf[par, :, 0:n] += jnp.sum((p * inv).reshape(4, 8, n), axis=0)
            return total

        t_buf[par, :, 0:n] = jnp.zeros((8, n), F32)
        lax.fori_loop(0, 8, softmax_rows, 0, unroll=2)

        tail = x[:, 512:640]
        low = pltpu.roll(dot(even, tail), 64, 1)
        queries = jnp.where(l128 < 64, low, dot(odd, tail)).astype(BF16)
        wtable = dot(spread, wtab[g], HIGHEST)
        wcol = jnp.sum(jnp.where(l128 == hl * 4 + v128 % 4, wtable, 0.0), axis=1, keepdims=True)
        row8, lane8 = (iota((8, 128), 0) // 2) % 2, iota((8, 128), 1)
        token = jnp.broadcast_to(wtab[g, 0:1, :], (8, 128))
        token = jnp.sum(jnp.where(lane8 == 8 + hl * 2 + row8, token, 0.0), axis=1, keepdims=True)
        for kb in range(b + 1):
            cols = slice(kb * BLK, kb * BLK + BLK)
            relu = jnp.maximum(dot_t(queries, keys[cols, 640:768]) * SCALE_INDEX, 0.0)
            r_buf[par, :, cols] = relu
            l_buf[par, :, cols] = jnp.sum((relu * wcol).reshape(16, 8, BLK), axis=0)
        target = dot(fold_t, t_buf[par, :, 0:n], HIGHEST)
        logits = dot(fold_l, l_buf[par, :, 0:n], HIGHEST)
        visible = iota((8, n), 1) - (iota((8, n), 0) // 2) % 2 <= e2 + b * BLK
        logits = jnp.where(visible, logits, NEG)
        top = jnp.max(logits, axis=1, keepdims=True)
        expo = jnp.exp(logits - top)
        probs = expo / jnp.sum(expo, axis=1, keepdims=True)
        l_buf[par, :, 0:n] = token * (probs - target)

        queries_t = queries.T
        wscaled = wcol * SCALE_INDEX
        gq_sum = jnp.zeros((128, 128), F32)
        gw_sum = jnp.zeros((128, 128), F32)
        for kb in range(b + 1):
            cols = slice(kb * BLK, kb * BLK + BLK)
            relu = r_buf[par, :, cols]
            dl = jnp.broadcast_to(l_buf[par, :, cols][None], (16, 8, BLK)).reshape(128, BLK)
            gwp = dl * relu
            gw_sum = gw_sum + gwp[:, 0:128] + gwp[:, 128:256]
            grad = jnp.where(relu > 0.0, dl * wscaled, 0.0).astype(BF16)
            gq_sum = gq_sum + dot(grad, keys[cols, 640:768])
            part = dot(queries_t, grad)
            if kb == b:
                gkt[:, cols] = part
            else:
                gkt[:, cols] += part
        gq[h] = gq_sum
        gws = jnp.sum(gw_sum, axis=1, keepdims=True)
        gwtab[g] += dot(gather, jnp.where(l128 == hl * 4 + v128 % 4, gws, 0.0), HIGHEST)

    gw[...] = gwtab[...].reshape(4, 32, 1, 128)
    gk[...] = gkt[...].T


def compute(meta, recv, wrecv, keys):
    vmem = pl.BlockSpec(memory_space=pltpu.VMEM)
    return pl.pallas_call(
        compute_kernel,
        in_specs=[pl.BlockSpec(memory_space=pltpu.SMEM), vmem, vmem, vmem],
        out_specs=(vmem, vmem, vmem),
        scratch_shapes=[
            pltpu.VMEM((2, 256, 2048), F32),
            pltpu.VMEM((2, 128, 2048), F32),
            pltpu.VMEM((128, 2048), F32),
            pltpu.VMEM((2, 8, 2048), F32),
            pltpu.VMEM((2, 8, 2048), F32),
            pltpu.VMEM((4, 32, 128), F32),
            pltpu.VMEM((4, 32, 128), F32),
        ],
        out_shape=(
            jax.ShapeDtypeStruct((8, 128, 128), F32),
            jax.ShapeDtypeStruct((4, 32, 1, 128), F32),
            jax.ShapeDtypeStruct((2048, 128), F32),
        ),
        compiler_params=pltpu.CompilerParams(vmem_limit_bytes=40 * 1024 * 1024),
        name="compute",
    )(meta, recv, wrecv, keys)


def return_kernel(
    gq, gw, gk, gq_out, gw_out, gk_out, rc, v1, rx, v2, ry, v3, rz, qs, qr, ws, wr, rss, rsr
):
    p = Place()
    barrier = enter(p)
    pair = pl.ds(p.group * 2, 2)
    pltpu.make_async_copy(gq.at[pair, p.heads], gq_out.at[:, p.flat], qr).start()
    pltpu.make_async_copy(gw.at[p.group, p.heads], gw_out.at[p.flat], wr).start()
    pl.semaphore_wait(barrier, 127)

    def remote(phase, j, src, dst, o):
        return pltpu.make_async_remote_copy(
            src_ref=src,
            dst_ref=dst,
            send_sem=rss.at[phase, j],
            recv_sem=rsr.at[phase, j],
            device_id=dev(*p.at(o)),
            device_id_type=MESH,
        )

    def send(o):
        heads, group = p.at(o)
        for source, target, ssem, rsem in (
            (gq.at[pl.ds(group * 2, 2), heads], gq_out.at[:, p.flat], qs, qr),
            (gw.at[group, heads], gw_out.at[p.flat], ws, wr),
        ):
            pltpu.make_async_remote_copy(
                src_ref=source,
                dst_ref=target,
                send_sem=ssem,
                recv_sem=rsem,
                device_id=dev(heads, group),
                device_id_type=MESH,
            ).start()

    core = remote(0, 0, gk.at[:, :, :, :, p.c[1]], rc, (0, 0, 0, 1))
    core.start()
    for o in ORDER[0:40]:
        send(o)
    core.wait()
    for color in range(2):
        half = slice(color * 8, color * 8 + 8)
        for x in range(4):
            v1[color, :, x] = gk[:, x % 2, :, x // 2, p.c[0], half] + rc[:, x % 2, :, x // 2, half]
    phase = []
    for j in range(1, 4):
        phase.append(remote(1, j - 1, v1.at[0, :, p.x[j]], rx.at[0, j - 1], (j, 0, 0, 0)))
        phase.append(remote(1, j + 2, v1.at[1, p.y[j]], rx.at[1, j - 1], (0, j, 0, 0)))
    for cp in phase:
        cp.start()
    for o in ORDER[40:90]:
        send(o)
    for cp in phase:
        cp.wait()
    v2[0] = v1[0, :, p.x[0]] + rx[0, 0] + rx[0, 1] + rx[0, 2]
    v2[1] = v1[1, p.y[0]] + rx[1, 0] + rx[1, 1] + rx[1, 2]
    phase = []
    for j in range(1, 4):
        phase.append(remote(2, j - 1, v2.at[0, p.y[j]], ry.at[0, j - 1], (0, j, 0, 0)))
        phase.append(remote(2, j + 2, v2.at[1, :, p.z[j]], ry.at[1, j - 1], (0, 0, j, 0)))
    for cp in phase:
        cp.start()
    for o in ORDER[90:127]:
        send(o)
    for cp in phase:
        cp.wait()
    v3[0] = v2[0, p.y[0]] + ry[0, 0] + ry[0, 1] + ry[0, 2]
    v3[1] = v2[1, :, p.z[0]] + ry[1, 0] + ry[1, 1] + ry[1, 2]
    phase = []
    for j in range(1, 4):
        phase.append(remote(3, j - 1, v3.at[0, p.z[j]], rz.at[0, j - 1], (0, 0, j, 0)))
        phase.append(remote(3, j + 2, v3.at[1, p.x[j]], rz.at[1, j - 1], (j, 0, 0, 0)))
    for cp in phase:
        cp.start()
    for cp in phase:
        cp.wait()
    gk_out[0:8] = v3[0, p.z[0]] + rz[0, 0] + rz[0, 1] + rz[0, 2]
    gk_out[8:16] = v3[1, p.x[0]] + rz[1, 0] + rz[1, 1] + rz[1, 2]
    pltpu.make_async_copy(gq_out, gq_out, qr).wait()
    pltpu.make_async_copy(gw_out, gw_out, wr).wait()
    part = gq_out.at[:, pl.ds(0, 127)]
    pltpu.make_async_copy(part, part, qs).wait()
    part = gw_out.at[pl.ds(0, 127)]
    pltpu.make_async_copy(part, part, ws).wait()


def send_back(gq, gw, gk):
    any_spec = pl.BlockSpec(memory_space=pl.ANY)
    vmem = pl.BlockSpec(memory_space=pltpu.VMEM)
    return pl.pallas_call(
        return_kernel,
        out_shape=(
            jax.ShapeDtypeStruct((2, 128, 4, 128), F32),
            jax.ShapeDtypeStruct((128, 1, 128), F32),
            jax.ShapeDtypeStruct((16, 128), F32),
        ),
        in_specs=[vmem] * 3,
        out_specs=(vmem,) * 3,
        scratch_shapes=[
            pltpu.VMEM((4, 2, 4, 2, 16, 128), F32),
            pltpu.VMEM((2, 4, 4, 4, 8, 128), F32),
            pltpu.VMEM((2, 3, 4, 4, 8, 128), F32),
            pltpu.VMEM((2, 4, 4, 8, 128), F32),
            pltpu.VMEM((2, 3, 4, 8, 128), F32),
            pltpu.VMEM((2, 4, 8, 128), F32),
            pltpu.VMEM((2, 3, 8, 128), F32),
            pltpu.SemaphoreType.DMA,
            pltpu.SemaphoreType.DMA,
            pltpu.SemaphoreType.DMA,
            pltpu.SemaphoreType.DMA,
            pltpu.SemaphoreType.DMA((4, 6)),
            pltpu.SemaphoreType.DMA((4, 6)),
        ],
        compiler_params=pltpu.CompilerParams(has_side_effects=True, collective_id=2),
        name="send_back",
    )(gq, gw, gk)


def on_device(q_main, latent, q_index, head_weight, k_index, token_weight, block_order):
    packed, wsend, mykeys = pack(q_main, q_index, head_weight, token_weight, latent, k_index)
    recv, wrecv, keys = exchange(packed, wsend, mykeys)
    flat = lax.axis_index("heads") * 4 + lax.axis_index("qgrp")
    place = jnp.arange(8, dtype=jnp.int32)
    where = jnp.sum(jnp.where(block_order[None, :] == place[:, None], place[None, :], 0), axis=1)
    meta = jnp.concatenate([where, flat[None]]).astype(jnp.int32)
    gq, gw, gk = compute(meta, recv.reshape(8, 256, 640), wrecv, keys.reshape(2048, 768))
    gq_out, gw_out, gk_out = send_back(
        gq.reshape(8, 32, 4, 128), gw, gk.reshape(4, 2, 4, 2, 2, 16, 128)
    )
    grad_q = gq_out.reshape(512, 2, 128)
    grad_w = gw_out[:, 0, 0:8].reshape(128, 2, 2, 2).transpose(3, 1, 0, 2).reshape(2, 512)
    return grad_q, grad_w, gk_out


def solution(mesh):
    return jax.shard_map(
        on_device,
        mesh=mesh,
        in_specs=(
            P("qgrp", "heads", None),
            P(("heads", "qgrp"), None),
            P("qgrp", "heads", None),
            P("heads", "qgrp"),
            P(("heads", "qgrp"), None),
            P("qgrp"),
            P(),
        ),
        out_specs=(P("qgrp", "heads", None), P("heads", "qgrp"), P(("heads", "qgrp"), None)),
        check_vma=False,
    )
```

```python
import math
import random

import jax
import jax.numpy as jnp
from jax import lax
from jax.experimental import pallas as pl
from jax.experimental.pallas import tpu as pltpu
from jax.sharding import PartitionSpec as P

MESH = pl.DeviceIdType.MESH
SCALE_INDEX = 128.0 ** (-0.5)
EXP_SCALE = 192.0 ** (-0.5) * math.log2(math.e)
NEG = -3.0e38
BLK = 256
F32 = jnp.float32
BF16 = jnp.bfloat16
HIGHEST = lax.Precision.HIGHEST


def far_first():
    every = [(a, b, c, d) for a in range(4) for b in range(4) for c in range(4) for d in range(2)][1:]
    random.Random(1).shuffle(every)
    return sorted(every, key=lambda o: sum(min(v, 4 - v) for v in o[:3]) + o[3] * 0.5)[::-1]


ORDER = far_first()
KEY_CUTS = (0, 16, 40, 80, 127)


class Place:
    def __init__(self):
        h = lax.axis_index("heads")
        q = lax.axis_index("qgrp")
        self.y = [lax.rem(lax.div(h, 8) + k, 4) for k in range(4)]
        self.z = [lax.rem(lax.rem(h, 4) + k, 4) for k in range(4)]
        x = lax.div(q, 2) * 2 + lax.rem(lax.div(h, 4), 2)
        self.x = [lax.rem(x + k, 4) for k in range(4)]
        self.c = [lax.rem(q, 2), 1 - lax.rem(q, 2)]
        self.x_low = [lax.rem(v, 2) for v in self.x]
        self.x_high = [lax.div(v, 2) for v in self.x]
        self.y8 = [v * 8 for v in self.y]
        self.xl4 = [v * 4 for v in self.x_low]
        self.xh2 = [v * 2 for v in self.x_high]
        self.heads, self.group = self.at((0, 0, 0, 0))
        self.flat = self.heads * 4 + self.group

    def at(self, o):
        dx, dy, dz, dc = o
        return self.y8[dy] + self.xl4[dx] + self.z[dz], self.xh2[dx] + self.c[dc]


def dev(heads, group):
    return {"heads": heads, "qgrp": group}


def enter(place):
    sem = pltpu.get_barrier_semaphore()
    for o in ORDER:
        pl.semaphore_signal(sem, inc=1, device_id=dev(*place.at(o)), device_id_type=MESH)
    return sem


def iota(shape, dim):
    return lax.broadcasted_iota(jnp.int32, shape, dim)


def dot_t(a, b, precision=None):
    return lax.dot_general(
        a, b, (((1,), (1,)), ((), ())), precision=precision, preferred_element_type=F32
    )


def dot(a, b, precision=None):
    return jnp.dot(a, b, precision=precision, preferred_element_type=F32)


def one_hot(mask):
    return jnp.where(mask, 1.0, 0.0)


def pack_kernel(main, index, weight, token, latent, key, packed, wsend, mykeys, perm, pick):
    @pl.when(pl.program_id(0) == 0)
    def _():
        out, src = iota((512, 512), 0), iota((512, 512), 1)
        perm[...] = one_hot(out == (src % 128) * 4 + src // 128).astype(BF16)
        out, src = iota((512, 256), 0), iota((512, 256), 1)
        pick[...] = one_hot(src == out // 2).astype(BF16)

    both = jnp.concatenate([main[h] for h in range(4)], axis=1)
    rows = dot_t(perm[...], both)
    tail = dot(pick[...], index[...])
    lane, row = iota((512, 128), 1), iota((512, 128), 0)
    tail = jnp.where(row % 2 == 0, pltpu.roll(tail, 64, 1), tail)
    last = jnp.concatenate([rows[:, 512:576], jnp.zeros((512, 64), F32)], axis=1)
    last = jnp.where(lane < 64, last, tail)
    full = jnp.concatenate([rows[:, 0:512], last], axis=1).astype(BF16)
    packed[0] = full.reshape(64, 8, 640)

    @pl.when(pl.program_id(0) == 0)
    def _():
        total = jnp.zeros((128, 128), F32)
        sub = iota((128, 256), 0)
        for hl in range(2):
            cols = slice(hl * 256, hl * 256 + 256)
            for i in range(2):
                table = jnp.zeros((128, 256), F32)
                for at, line in (
                    (hl * 4 + i * 2, weight[0:1, cols]),
                    (hl * 4 + i * 2 + 1, weight[1:2, cols]),
                    (8 + hl * 2 + i, token[0:1, cols]),
                ):
                    table = jnp.where(sub == at, jnp.broadcast_to(line, (128, 256)), table)
                choose = one_hot(iota((128, 256), 1) == iota((128, 256), 0) * 2 + i)
                total = total + dot_t(choose, table, HIGHEST)
        wsend[...] = total.reshape(128, 1, 128)
        mykeys[:, 0:576] = latent[...]
        mykeys[:, 576:640] = jnp.zeros((16, 64), BF16)
        mykeys[:, 640:768] = key[...]


def pack(q_main, q_index, head_weight, token_weight, latent, k_index):
    return pl.pallas_call(
        pack_kernel,
        grid=(4,),
        in_specs=[
            pl.BlockSpec((4, 576, 128), lambda t: (0, 0, t)),
            pl.BlockSpec((256, 128), lambda t: (t, 0)),
            pl.BlockSpec((2, 512), lambda t: (0, 0)),
            pl.BlockSpec((1, 512), lambda t: (0, 0)),
            pl.BlockSpec((16, 576), lambda t: (0, 0)),
            pl.BlockSpec((16, 128), lambda t: (0, 0)),
        ],
        out_specs=(
            pl.BlockSpec((1, 64, 8, 640), lambda t: (t // 2, t % 2, 0, 0)),
            pl.BlockSpec((128, 1, 128), lambda t: (0, 0, 0)),
            pl.BlockSpec((16, 768), lambda t: (0, 0)),
        ),
        out_shape=(
            jax.ShapeDtypeStruct((2, 128, 8, 640), BF16),
            jax.ShapeDtypeStruct((128, 1, 128), F32),
            jax.ShapeDtypeStruct((16, 768), BF16),
        ),
        scratch_shapes=[pltpu.VMEM((512, 512), BF16), pltpu.VMEM((512, 256), BF16)],
        name="pack",
    )(
        jnp.transpose(q_main, (1, 2, 0)),
        q_index.reshape(1024, 128),
        head_weight,
        token_weight.reshape(1, 512),
        latent,
        k_index,
    )


PARTS = ((0, 2), (1, 3))


def fused_kernel(
    meta,
    packed,
    wsend,
    mykeys,
    gq_out,
    gw_out,
    gk_out,
    recv0,
    recv1,
    wrecv,
    keys,
    s_buf,
    r_buf,
    t_buf,
    l_buf,
    gkt,
    gq_block,
    gw_block,
    gq,
    gw,
    gkb,
    rc,
    v1,
    rx,
    v2,
    ry,
    v3,
    rz,
    qs,
    qr,
    ws,
    wr,
    ls,
    ags,
    agr,
    cs,
    cr,
    xs,
    xr,
    rs,
    rr,
    bs,
    br,
    us,
    ur,
):
    p = Place()
    barrier = enter(p)
    recv = (recv0, recv1)
    mine = pl.ds(p.group * 2, 2)
    base = p.y[0] * 4 + p.x_low[0] * 2

    def remote(src, dst, ssem, rsem, o):
        return pltpu.make_async_remote_copy(
            src_ref=src,
            dst_ref=dst,
            send_sem=ssem,
            recv_sem=rsem,
            device_id=dev(*p.at(o)),
            device_id_type=MESH,
        )

    def key_phase(number):
        copies = []
        for color, axes in enumerate(("zyx", "yxz", "xzy")):
            done = axes[:number]
            ref = keys.at[
                slice(None) if "y" in done else p.y[0],
                slice(None) if "x" in done else p.x_low[0],
                slice(None) if "z" in done else p.z[0],
                slice(None) if "x" in done else p.x_high[0],
                p.c[0],
                slice(None),
                pl.ds(color * 256, 256),
            ]
            for j in range(1, 4):
                o = tuple(j if axis == axes[number] else 0 for axis in "xyz") + (0,)
                at = color * 3 + j - 1
                copies.append(remote(ref, ref, ags.at[number, at], agr.at[number, at], o))
        return copies

    def core_phase():
        ref = keys.at[:, :, :, :, p.c[0]]
        return [remote(ref, ref, ags.at[3, 0], agr.at[3, 0], (0, 0, 0, 1))]

    def send(o):
        heads, group = p.at(o)
        e = heads * 4 + group
        part, slot = o[2] % 2, o[2] // 2
        remote(packed.at[:, e], recv[part].at[mine, base + slot], qs, qr.at[part], o).start()
        remote(wsend.at[e], wrecv.at[p.group, part * 16 + base + slot], ws, wr, o).start()

    own = pltpu.make_async_copy(mykeys, keys.at[p.y[0], p.x_low[0], p.z[0], p.x_high[0], p.c[0]], ls)
    own.start()
    pltpu.make_async_copy(packed.at[:, p.flat], recv0.at[mine, base], qr.at[0]).start()
    pltpu.make_async_copy(wsend.at[p.flat], wrecv.at[p.group, base], wr).start()
    own.wait()
    pl.semaphore_wait(barrier, 127)
    order = [o for part in PARTS for o in ORDER if o[2] in part]
    for number in range(4):
        phase = key_phase(number) if number < 3 else core_phase()
        for cp in phase:
            cp.start()
        for o in order[KEY_CUTS[number] : KEY_CUTS[number + 1]]:
            send(o)
        for cp in phase:
            cp.wait()

    e2 = p.flat * 2
    spread = one_hot(iota((64, 16), 1) == iota((64, 16), 0) // 4)
    gather = one_hot(iota((32, 128), 1) // 4 == iota((32, 128), 0))
    even = one_hot(iota((64, 128), 1) == iota((64, 128), 0) * 2).astype(BF16)
    odd = one_hot(iota((64, 128), 1) == iota((64, 128), 0) * 2 + 1).astype(BF16)
    f_out, f_in = iota((8, 8), 0), iota((8, 8), 1)
    fold_t = one_hot(f_in // 4 == (f_out // 2) % 2)
    fold_l = one_hot((f_in // 2) % 2 == (f_out // 2) % 2)
    l64, v64 = iota((64, 128), 1), iota((64, 128), 0)
    l128, v128 = iota((128, 128), 1), iota((128, 128), 0)
    row8, lane8 = (iota((8, 128), 0) // 2) % 2, iota((8, 128), 1)

    def half_of(b):
        h = meta[b]
        return h, lax.div(h, 2), lax.rem(h, 2)

    def index_queries(part, h):
        tail = recv[part][h, :, :, 512:640].reshape(128, 128)
        low = pltpu.roll(dot(even, tail), 64, 1)
        return jnp.where(l64 < 64, low, dot(odd, tail)).astype(BF16)

    def weight_column(part, g, hl):
        table = dot(spread, wrecv[g, pl.ds(part * 16, 16), 0, :], HIGHEST)
        return jnp.sum(jnp.where(l64 == hl * 4 + v64 % 4, table, 0.0), axis=1, keepdims=True)

    def key_block(kb):
        return keys[kb // 2, kb % 2].reshape(256, 768)

    def forward(part):
        for b in range(7, -1, -1):
            n = (b + 1) * BLK
            par = b % 2
            h, g, hl = half_of(b)
            x = recv[part][h].reshape(128, 640)
            for kb in range(b + 1):
                cols = slice(kb * BLK, kb * BLK + BLK)
                s = dot_t(x, key_block(kb)[:, 0:640])
                if kb == b:
                    row = (iota((128, BLK), 0) % 8) // 4
                    s = jnp.where(iota((128, BLK), 1) - row <= e2, s, NEG)
                s_buf[par, :, cols] = s

            def softmax_rows(r, total):
                rows = pl.ds(pl.multiple_of(r * 32, 32), 32)
                s = s_buf[par, rows, 0:n]
                top = jnp.max(s, axis=1, keepdims=True)
                w = jnp.exp2((s - top) * EXP_SCALE)
                inv = (1.0 / 128.0) / jnp.sum(w, axis=1, keepdims=True)
                t_buf[b, :, 0:n] += jnp.sum((w * inv).reshape(4, 8, n), axis=0)
                return total

            if part == 0:
                t_buf[b, :, 0:n] = jnp.zeros((8, n), F32)
            lax.fori_loop(0, 4, softmax_rows, 0, unroll=2)

            queries = index_queries(part, h)
            wcol = weight_column(part, g, hl)
            for kb in range(b + 1):
                cols = slice(kb * BLK, kb * BLK + BLK)
                relu = jnp.maximum(dot_t(queries, key_block(kb)[:, 640:768]) * SCALE_INDEX, 0.0)
                r_buf[b, part * 64 : part * 64 + 64, cols] = relu
                add = jnp.sum((relu * wcol).reshape(8, 8, BLK), axis=0)
                if part == 0:
                    l_buf[b, :, cols] = add
                else:
                    l_buf[b, :, cols] += add

    def reduce_x(y):
        for b in (2 * y + 1, 2 * y):
            cp = remote(gkb.at[b, :, :, p.c[1]], rc.at[b], cs.at[b], cr.at[b], (0, 0, 0, 1))
            cp.wait()
        for x in range(4):
            b = 2 * y + x % 2
            v1[y, x] = gkb[b, :, x // 2, p.c[0]] + rc[b, :, x // 2]
        for cp in x_copies(y):
            cp.start()

    def x_copies(y):
        return [
            remote(v1.at[y, p.x[j]], rx.at[y, j - 1], xs.at[y, j - 1], xr.at[y, j - 1], (j, 0, 0, 0))
            for j in range(1, 4)
        ]

    pltpu.make_async_copy(recv0, recv0, qr.at[0]).wait()
    pltpu.make_async_copy(wrecv, wrecv, wr).wait()
    forward(0)
    pltpu.make_async_copy(recv1, recv1, qr.at[1]).wait()
    forward(1)

    gkt[...] = jnp.zeros_like(gkt)
    for b in range(7, -1, -1):
        n = (b + 1) * BLK
        h, g, hl = half_of(b)
        target = dot(fold_t, t_buf[b, :, 0:n], HIGHEST)
        logits = dot(fold_l, l_buf[b, :, 0:n], HIGHEST)
        visible = iota((8, n), 1) - (iota((8, n), 0) // 2) % 2 <= e2 + b * BLK
        logits = jnp.where(visible, logits, NEG)
        top = jnp.max(logits, axis=1, keepdims=True)
        expo = jnp.exp(logits - top)
        probs = expo / jnp.sum(expo, axis=1, keepdims=True)
        token = jnp.broadcast_to(wrecv[g, 0], (8, 128))
        token = jnp.sum(jnp.where(lane8 == 8 + hl * 2 + row8, token, 0.0), axis=1, keepdims=True)
        l_buf[b, :, 0:n] = token * (probs - target)

        queries = jnp.concatenate([index_queries(part, h) for part in range(2)], axis=0)
        wcol = jnp.concatenate([weight_column(part, g, hl) for part in range(2)], axis=0)
        queries_t = queries.T
        wscaled = wcol * SCALE_INDEX
        gq_sum = jnp.zeros((128, 128), F32)
        gw_sum = jnp.zeros((128, 128), F32)
        for kb in range(b + 1):
            cols = slice(kb * BLK, kb * BLK + BLK)
            relu = r_buf[b, :, cols]
            dl = jnp.broadcast_to(l_buf[b, :, cols][None], (16, 8, BLK)).reshape(128, BLK)
            gwp = dl * relu
            gw_sum = gw_sum + gwp[:, 0:128] + gwp[:, 128:256]
            grad = jnp.where(relu > 0.0, dl * wscaled, 0.0).astype(BF16)
            gq_sum = gq_sum + dot(grad, key_block(kb)[:, 640:768])
            gkt[:, cols] += dot(queries_t, grad)
        gq_block[b] = gq_sum.astype(GQ)
        gws = jnp.sum(gw_sum, axis=1, keepdims=True)
        gw_block[b] = dot(gather, jnp.where(l128 == hl * 4 + v128 % 4, gws, 0.0), HIGHEST)
        gkb[b] = gkt[:, b * BLK : b * BLK + BLK].T.reshape(4, 2, 2, 16, 128)
        remote(gkb.at[b, :, :, p.c[1]], rc.at[b], cs.at[b], cr.at[b], (0, 0, 0, 1)).start()
        if b % 2 == 1 and b < 7:
            reduce_x((b + 1) // 2)

    for h in range(8):
        gq[h] = gq_block[meta[8 + h]].reshape(32, 4, 128)
    for g in range(4):
        total = gw_block[meta[8 + 2 * g]] + gw_block[meta[9 + 2 * g]]
        gw[g] = total.reshape(32, 1, 128)
    reduce_x(0)

    def returned(o):
        heads, group = p.at(o)
        back = (4 - o[2]) % 4
        slot = (back % 2) * 16 + p.y8[o[1]] // 2 + p.x_low[o[0]] * 2 + back // 2
        remote(gq.at[pl.ds(group * 2, 2), slot], gq_out.at[:, p.flat], bs, br, o).start()
        remote(gw.at[group, slot], gw_out.at[p.flat], us, ur, o).start()

    pltpu.make_async_copy(gq.at[mine, base], gq_out.at[:, p.flat], br).start()
    pltpu.make_async_copy(gw.at[p.group, base], gw_out.at[p.flat], ur).start()
    for o in ORDER[0:BACK_CUT]:
        returned(o)
    for y in range(4):
        for cp in x_copies(y):
            cp.wait()
    for y in range(4):
        v2[y] = v1[y, p.x[0]] + rx[y, 0] + rx[y, 1] + rx[y, 2]
    phase = [
        remote(v2.at[p.y[j]], ry.at[j - 1], rs.at[0, j - 1], rr.at[0, j - 1], (0, j, 0, 0))
        for j in range(1, 4)
    ]
    for cp in phase:
        cp.start()
    for o in ORDER[BACK_CUT:127]:
        returned(o)
    for cp in phase:
        cp.wait()
    v3[...] = v2[p.y[0]] + ry[0] + ry[1] + ry[2]
    phase = [
        remote(v3.at[p.z[j]], rz.at[j - 1], rs.at[1, j - 1], rr.at[1, j - 1], (0, 0, j, 0))
        for j in range(1, 4)
    ]
    for cp in phase:
        cp.start()
    for cp in phase:
        cp.wait()
    gk_out[...] = v3[p.z[0]] + rz[0] + rz[1] + rz[2]
    pltpu.make_async_copy(gq_out, gq_out, br).wait()
    pltpu.make_async_copy(gw_out, gw_out, ur).wait()
    for ref, sem in ((packed, qs), (gq_out, bs)):
        part = ref.at[:, pl.ds(0, 127)]
        pltpu.make_async_copy(part, part, sem).wait()
    for ref, sem in ((wsend, ws), (gw_out, us)):
        part = ref.at[pl.ds(0, 127)]
        pltpu.make_async_copy(part, part, sem).wait()


GQ = BF16
BACK_CUT = 60


def fused(meta, packed, wsend, mykeys):
    any_spec = pl.BlockSpec(memory_space=pl.ANY)
    vmem = pl.BlockSpec(memory_space=pltpu.VMEM)
    sem = pltpu.SemaphoreType.DMA
    return pl.pallas_call(
        fused_kernel,
        in_specs=[pl.BlockSpec(memory_space=pltpu.SMEM), any_spec, any_spec, any_spec],
        out_specs=(any_spec, any_spec, vmem),
        out_shape=(
            jax.ShapeDtypeStruct((2, 128, 4, 128), GQ),
            jax.ShapeDtypeStruct((128, 1, 128), F32),
            jax.ShapeDtypeStruct((16, 128), F32),
        ),
        scratch_shapes=[
            pltpu.VMEM((8, 16, 8, 640), BF16),
            pltpu.VMEM((8, 16, 8, 640), BF16),
            pltpu.VMEM((4, 32, 1, 128), F32),
            pltpu.VMEM((4, 2, 4, 2, 2, 16, 768), BF16),
            pltpu.VMEM((2, 128, 2048), F32),
            pltpu.VMEM((8, 128, 2048), F32),
            pltpu.VMEM((8, 8, 2048), F32),
            pltpu.VMEM((8, 8, 2048), F32),
            pltpu.VMEM((128, 2048), F32),
            pltpu.VMEM((8, 128, 128), GQ),
            pltpu.VMEM((8, 32, 128), F32),
            pltpu.VMEM((8, 32, 4, 128), GQ),
            pltpu.VMEM((4, 32, 1, 128), F32),
            pltpu.VMEM((8, 4, 2, 2, 16, 128), F32),
            pltpu.VMEM((8, 4, 2, 16, 128), F32),
            pltpu.VMEM((4, 4, 4, 16, 128), F32),
            pltpu.VMEM((4, 3, 4, 16, 128), F32),
            pltpu.VMEM((4, 4, 16, 128), F32),
            pltpu.VMEM((3, 4, 16, 128), F32),
            pltpu.VMEM((4, 16, 128), F32),
            pltpu.VMEM((3, 16, 128), F32),
            sem,
            sem((2,)),
            sem,
            sem,
            sem,
            sem((4, 9)),
            sem((4, 9)),
            sem((8,)),
            sem((8,)),
            sem((4, 3)),
            sem((4, 3)),
            sem((2, 3)),
            sem((2, 3)),
            sem,
            sem,
            sem,
            sem,
        ],
        compiler_params=pltpu.CompilerParams(
            has_side_effects=True, collective_id=1, vmem_limit_bytes=48 * 1024 * 1024
        ),
        name="fused",
    )(meta, packed, wsend, mykeys)


def on_device(q_main, latent, q_index, head_weight, k_index, token_weight, block_order):
    packed, wsend, mykeys = pack(q_main, q_index, head_weight, token_weight, latent, k_index)
    place = jnp.arange(8, dtype=jnp.int32)
    where = jnp.sum(jnp.where(block_order[None, :] == place[:, None], place[None, :], 0), axis=1)
    meta = jnp.concatenate([where, block_order]).astype(jnp.int32)
    gq, gw, gk = fused(meta, packed, wsend, mykeys)
    grad_q = gq.astype(F32).reshape(512, 2, 128)
    grad_w = gw[:, 0, 0:8].reshape(128, 2, 2, 2).transpose(3, 1, 0, 2).reshape(2, 512)
    return grad_q, grad_w, gk


def solution(mesh):
    return jax.shard_map(
        on_device,
        mesh=mesh,
        in_specs=(
            P("qgrp", "heads", None),
            P(("heads", "qgrp"), None),
            P("qgrp", "heads", None),
            P("heads", "qgrp"),
            P(("heads", "qgrp"), None),
            P("qgrp"),
            P(),
        ),
        out_specs=(P("qgrp", "heads", None), P("heads", "qgrp"), P(("heads", "qgrp"), None)),
        check_vma=False,
    )
```

```python
import math
import random

import jax
import jax.numpy as jnp
from jax import lax
from jax.experimental import pallas as pl
from jax.experimental.pallas import tpu as pltpu
from jax.sharding import PartitionSpec as P

MESH = pl.DeviceIdType.MESH
SCALE_INDEX = 128.0 ** (-0.5)
EXP_SCALE = 192.0 ** (-0.5) * math.log2(math.e)
NEG = -3.0e38
BLK = 256
F32 = jnp.float32
BF16 = jnp.bfloat16
HIGHEST = lax.Precision.HIGHEST


def far_first():
    every = [(a, b, c, d) for a in range(4) for b in range(4) for c in range(4) for d in range(2)][1:]
    random.Random(1).shuffle(every)
    return sorted(every, key=lambda o: sum(min(v, 4 - v) for v in o[:3]) + o[3] * 0.5)[::-1]


ORDER = far_first()
KEY_CUTS = (0, 16, 40, 80, 127)


class Place:
    def __init__(self):
        h = lax.axis_index("heads")
        q = lax.axis_index("qgrp")
        self.y = [lax.rem(lax.div(h, 8) + k, 4) for k in range(4)]
        self.z = [lax.rem(lax.rem(h, 4) + k, 4) for k in range(4)]
        x = lax.div(q, 2) * 2 + lax.rem(lax.div(h, 4), 2)
        self.x = [lax.rem(x + k, 4) for k in range(4)]
        self.c = [lax.rem(q, 2), 1 - lax.rem(q, 2)]
        self.x_low = [lax.rem(v, 2) for v in self.x]
        self.x_high = [lax.div(v, 2) for v in self.x]
        self.y8 = [v * 8 for v in self.y]
        self.xl4 = [v * 4 for v in self.x_low]
        self.xh2 = [v * 2 for v in self.x_high]
        self.heads, self.group = self.at((0, 0, 0, 0))
        self.flat = self.heads * 4 + self.group

    def at(self, o):
        dx, dy, dz, dc = o
        return self.y8[dy] + self.xl4[dx] + self.z[dz], self.xh2[dx] + self.c[dc]


def dev(heads, group):
    return {"heads": heads, "qgrp": group}


def enter(place):
    sem = pltpu.get_barrier_semaphore()
    for o in ORDER:
        pl.semaphore_signal(sem, inc=1, device_id=dev(*place.at(o)), device_id_type=MESH)
    return sem


def iota(shape, dim):
    return lax.broadcasted_iota(jnp.int32, shape, dim)


def dot_t(a, b, precision=None):
    return lax.dot_general(
        a, b, (((1,), (1,)), ((), ())), precision=precision, preferred_element_type=F32
    )


def dot(a, b, precision=None):
    return jnp.dot(a, b, precision=precision, preferred_element_type=F32)


def one_hot(mask):
    return jnp.where(mask, 1.0, 0.0)


PARTS = ((0, 2), (1, 3))


def fused_kernel(
    order_ref,
    main_hbm,
    index_hbm,
    weight_hbm,
    token_hbm,
    latent_hbm,
    key_hbm,
    gq_out,
    gw_out,
    gk_out,
    main,
    index,
    weight,
    token_in,
    latent,
    key,
    perm,
    packed,
    wsend,
    gw_recv,
    recv0,
    recv1,
    wrecv,
    keys,
    s_buf,
    r_buf,
    t_buf,
    l_buf,
    gkt,
    gq_block,
    gw_block,
    gq,
    gw,
    gkb,
    rc,
    v1,
    rx,
    v2,
    rv,
    ms,
    qs,
    qr,
    ws,
    wr,
    ls,
    ags,
    agr,
    fs,
    fr,
    cs,
    cr,
    xs,
    xr,
    vs,
    vr,
    bs,
    br,
    us,
    ur,
):
    p = Place()
    tiles = [
        pltpu.make_async_copy(
            main_hbm.at[:, :, pl.ds(t * 128, 128)], main.at[:, :, pl.ds(t * 128, 128)], ms.at[t]
        )
        for t in range(4)
    ]
    small = [
        pltpu.make_async_copy(src, dst, ms.at[4 + at])
        for at, (src, dst) in enumerate(
            (
                (latent_hbm, latent),
                (key_hbm, key),
                (index_hbm, index),
                (weight_hbm, weight),
                (token_hbm, token_in),
            )
        )
    ]
    for cp in small[0:2] + tiles + small[2:]:
        cp.start()
    barrier = enter(p)
    recv = (recv0, recv1)
    mine = pl.ds(p.group * 2, 2)
    base = p.y[0] * 4 + p.x_low[0] * 2

    def remote(src, dst, ssem, rsem, o):
        return pltpu.make_async_remote_copy(
            src_ref=src,
            dst_ref=dst,
            send_sem=ssem,
            recv_sem=rsem,
            device_id=dev(*p.at(o)),
            device_id_type=MESH,
        )

    def key_phase(number):
        copies = []
        for color, axes in enumerate(("zyx", "yxz", "xzy")):
            done = axes[:number]
            ref = keys.at[
                color,
                slice(None) if "y" in done else p.y[0],
                slice(None) if "x" in done else p.x_low[0],
                slice(None) if "z" in done else p.z[0],
                slice(None) if "x" in done else p.x_high[0],
                p.c[0],
            ]
            for j in range(1, 4):
                o = tuple(j if axis == axes[number] else 0 for axis in "xyz") + (0,)
                at = color * 3 + j - 1
                copies.append(remote(ref, ref, ags.at[number, at], agr.at[number, at], o))
        return copies

    def to_partner(number, at, ref):
        return remote(ref, ref, fs.at[number, at], fr.at[number, at], (0, 0, 0, 1))

    def block(color, axes, number, o):
        done = axes[:number]
        return keys.at[
            color,
            slice(None) if "y" in done else p.y[-o[1] % 4],
            slice(None) if "x" in done else p.x_low[-o[0] % 4],
            slice(None) if "z" in done else p.z[-o[2] % 4],
            slice(None) if "x" in done else p.x_high[-o[0] % 4],
            p.c[0],
        ]

    def send(o):
        heads, group = p.at(o)
        e = heads * 4 + group
        part, slot = o[2] % 2, o[2] // 2
        remote(packed.at[:, e], recv[part].at[mine, base + slot], qs, qr.at[part], o).start()
        remote(wsend.at[e], wrecv.at[p.group, part * 16 + base + slot], ws, wr, o).start()

    def pack_tile(t):
        lanes = pl.ds(t * 128, 128)
        both = jnp.concatenate([main[h, :, lanes] for h in range(4)], axis=1)
        rows = dot_t(perm[:, 0:512], both)
        tail = dot(perm[:, 512:768], index[t * 256 : t * 256 + 256])
        lane, row = iota((512, 128), 1), iota((512, 128), 0)
        tail = jnp.where(row % 2 == 0, pltpu.roll(tail, 64, 1), tail)
        last = jnp.concatenate([rows[:, 512:576], jnp.zeros((512, 64), F32)], axis=1)
        last = jnp.where(lane < 64, last, tail)
        full = jnp.concatenate([rows[:, 0:512], last], axis=1).astype(BF16)
        packed[t // 2, (t % 2) * 64 : (t % 2) * 64 + 64] = full.reshape(64, 8, 640)

    def pack_weights():
        total = jnp.zeros((128, 128), F32)
        sub = iota((128, 256), 0)
        for hl in range(2):
            cols = slice(hl * 256, hl * 256 + 256)
            for i in range(2):
                table = jnp.zeros((128, 256), F32)
                for at, line in (
                    (hl * 4 + i * 2, weight[0:1, cols]),
                    (hl * 4 + i * 2 + 1, weight[1:2, cols]),
                    (8 + hl * 2 + i, token_in[0:1, cols]),
                ):
                    table = jnp.where(sub == at, jnp.broadcast_to(line, (128, 256)), table)
                choose = one_hot(iota((128, 256), 1) == iota((128, 256), 0) * 2 + i)
                total = total + dot_t(choose, table, HIGHEST)
        wsend[...] = total.reshape(128, 1, 128)

    small[0].wait()
    small[1].wait()
    at = (p.y[0], p.x_low[0], p.z[0], p.x_high[0], p.c[0])
    keys[(0,) + at] = latent[:, 0:256]
    keys[(1,) + at] = latent[:, 256:512]
    keys[(2,) + at] = jnp.concatenate([latent[:, 512:576], jnp.zeros((16, 64), BF16), key[...]], axis=1)
    out, src = iota((512, 512), 0), iota((512, 512), 1)
    perm[:, 0:512] = one_hot(out == (src % 128) * 4 + src // 128).astype(BF16)
    out, src = iota((512, 256), 0), iota((512, 256), 1)
    perm[:, 512:768] = one_hot(src == out // 2).astype(BF16)
    pl.semaphore_wait(barrier, 127)
    order = [o for part in PARTS for o in ORDER if o[2] in part]
    colors = list(enumerate(("zyx", "yxz", "xzy")))
    forwards = []
    for number in range(3):
        phase = key_phase(number)
        for cp in phase:
            cp.start()
        if number < 2:
            if number == 0:
                for cp in small[2:]:
                    cp.wait()
                pack_weights()
            for t in (2 * number, 2 * number + 1):
                tiles[t].wait()
                pack_tile(t)
        else:
            for color, axes in colors:
                cp = to_partner(color, 0, block(color, axes, 2, (0, 0, 0, 0)))
                cp.start()
                forwards.append(cp)
            pltpu.make_async_copy(packed.at[:, p.flat], recv0.at[mine, base], qr.at[0]).start()
            pltpu.make_async_copy(wsend.at[p.flat], wrecv.at[p.group, base], wr).start()
            for o in order:
                send(o)
        for j in range(1, 4):
            for color, axes in colors:
                phase[color * 3 + j - 1].wait()
                if number == 2:
                    o = tuple(j if axis == axes[2] else 0 for axis in "xyz")
                    cp = to_partner(color, j, block(color, axes, 2, o))
                    cp.start()
                    forwards.append(cp)
    for cp in forwards:
        cp.wait()

    e2 = p.flat * 2
    spread = one_hot(iota((64, 16), 1) == iota((64, 16), 0) // 4)
    gather = one_hot(iota((32, 128), 1) // 4 == iota((32, 128), 0))
    even = one_hot(iota((64, 128), 1) == iota((64, 128), 0) * 2).astype(BF16)
    odd = one_hot(iota((64, 128), 1) == iota((64, 128), 0) * 2 + 1).astype(BF16)
    f_out, f_in = iota((8, 8), 0), iota((8, 8), 1)
    fold_t = one_hot(f_in // 4 == (f_out // 2) % 2)
    fold_l = one_hot((f_in // 2) % 2 == (f_out // 2) % 2)
    l64, v64 = iota((64, 128), 1), iota((64, 128), 0)
    l128, v128 = iota((128, 128), 1), iota((128, 128), 0)
    row8, lane8 = (iota((8, 128), 0) // 2) % 2, iota((8, 128), 1)

    def half_of(b):
        h = 0
        for at in range(1, 8):
            h = jnp.where(order_ref[at] == b, at, h)
        return h, lax.div(h, 2), lax.rem(h, 2)

    def index_queries(part, h):
        tail = recv[part][h, :, :, 512:640].reshape(128, 128)
        low = pltpu.roll(dot(even, tail), 64, 1)
        return jnp.where(l64 < 64, low, dot(odd, tail)).astype(BF16)

    def weight_column(part, g, hl):
        table = dot(spread, wrecv[g, pl.ds(part * 16, 16), 0, :], HIGHEST)
        return jnp.sum(jnp.where(l64 == hl * 4 + v64 % 4, table, 0.0), axis=1, keepdims=True)

    def key_block(kb):
        parts = [keys[color, kb // 2, kb % 2].reshape(256, 256) for color in range(3)]
        return jnp.concatenate(parts, axis=1)

    def forward(part):
        for b in range(7, -1, -1):
            n = (b + 1) * BLK
            par = b % 2
            h, g, hl = half_of(b)
            x = recv[part][h].reshape(128, 640)
            for kb in range(b + 1):
                cols = slice(kb * BLK, kb * BLK + BLK)
                s = dot_t(x, key_block(kb)[:, 0:640])
                if kb == b:
                    row = (iota((128, BLK), 0) % 8) // 4
                    s = jnp.where(iota((128, BLK), 1) - row <= e2, s, NEG)
                s_buf[par, :, cols] = s

            def softmax_rows(r):
                rows = slice(r * 32, r * 32 + 32)
                s = s_buf[par, rows, 0:n]
                top = jnp.max(s, axis=1, keepdims=True)
                w = jnp.exp2((s - top) * EXP_SCALE)
                inv = (1.0 / 128.0) / jnp.sum(w, axis=1, keepdims=True)
                add = jnp.sum((w * inv).reshape(4, 8, n), axis=0)
                if part == 0 and r == 0:
                    t_buf[b, :, 0:n] = add
                else:
                    t_buf[b, :, 0:n] += add

            for r in range(4):
                softmax_rows(r)

            queries = index_queries(part, h)
            wcol = weight_column(part, g, hl)
            for kb in range(b + 1):
                cols = slice(kb * BLK, kb * BLK + BLK)
                relu = jnp.maximum(dot_t(queries, key_block(kb)[:, 640:768]) * SCALE_INDEX, 0.0)
                r_buf[b, part * 64 : part * 64 + 64, cols] = relu
                add = jnp.sum((relu * wcol).reshape(8, 8, BLK), axis=0)
                if part == 0:
                    l_buf[b, :, cols] = add
                else:
                    l_buf[b, :, cols] += add

    def reduce_x(y):
        for b in (2 * y + 1, 2 * y):
            cp = remote(gkb.at[b, :, :, p.c[1]], rc.at[b], cs.at[b], cr.at[b], (0, 0, 0, 1))
            cp.wait()
        for x in range(4):
            b = 2 * y + x % 2
            v1[y, x] = gkb[b, :, x // 2, p.c[0]] + rc[b, :, x // 2]
        for cp in x_copies(y):
            cp.start()

    def x_copies(y):
        return [
            remote(v1.at[y, p.x[j]], rx.at[y, j - 1], xs.at[y, j - 1], xr.at[y, j - 1], (j, 0, 0, 0))
            for j in range(1, 4)
        ]

    def plane_copy(y, j):
        slot = p.y[0] * 4 + p.z[0]
        return pltpu.make_async_remote_copy(
            src_ref=v2.at[y, p.z[j]],
            dst_ref=rv.at[slot],
            send_sem=vs.at[y, j],
            recv_sem=vr.at[slot],
            device_id=dev(y * 8 + p.xl4[0] + p.z[j], p.group),
            device_id_type=MESH,
        )

    def plane_each(y, action):
        for j in range(4):
            if j:
                action(plane_copy(y, j))
            else:

                @pl.when(p.y[0] != y)
                def _():
                    action(plane_copy(y, 0))

    def finish_x(y):
        for cp in x_copies(y):
            cp.wait()
        v2[y] = v1[y, p.x[0]] + rx[y, 0] + rx[y, 1] + rx[y, 2]
        plane_each(y, lambda cp: cp.start())

    pltpu.make_async_copy(recv0, recv0, qr.at[0]).wait()
    pltpu.make_async_copy(wrecv, wrecv, wr).wait()
    forward(0)
    pltpu.make_async_copy(recv1, recv1, qr.at[1]).wait()
    forward(1)

    gkt[...] = jnp.zeros_like(gkt)
    for b in range(7, -1, -1):
        n = (b + 1) * BLK
        h, g, hl = half_of(b)
        target = dot(fold_t, t_buf[b, :, 0:n], HIGHEST)
        logits = dot(fold_l, l_buf[b, :, 0:n], HIGHEST)
        visible = iota((8, n), 1) - (iota((8, n), 0) // 2) % 2 <= e2 + b * BLK
        logits = jnp.where(visible, logits, NEG)
        top = jnp.max(logits, axis=1, keepdims=True)
        expo = jnp.exp(logits - top)
        probs = expo / jnp.sum(expo, axis=1, keepdims=True)
        token = jnp.broadcast_to(wrecv[g, 0], (8, 128))
        token = jnp.sum(jnp.where(lane8 == 8 + hl * 2 + row8, token, 0.0), axis=1, keepdims=True)
        l_buf[b, :, 0:n] = token * (probs - target)

        queries = jnp.concatenate([index_queries(part, h) for part in range(2)], axis=0)
        wcol = jnp.concatenate([weight_column(part, g, hl) for part in range(2)], axis=0)
        queries_t = queries.T
        wscaled = wcol * SCALE_INDEX
        gq_sum = jnp.zeros((128, 128), F32)
        gw_sum = jnp.zeros((128, 128), F32)
        for kb in range(b + 1):
            cols = slice(kb * BLK, kb * BLK + BLK)
            relu = r_buf[b, :, cols]
            dl = jnp.broadcast_to(l_buf[b, :, cols][None], (16, 8, BLK)).reshape(128, BLK)
            gwp = dl * relu
            gw_sum = gw_sum + gwp[:, 0:128] + gwp[:, 128:256]
            grad = jnp.where(relu > 0.0, dl * wscaled, 0.0).astype(BF16)
            gq_sum = gq_sum + dot(grad, key_block(kb)[:, 640:768])
            gkt[:, cols] += dot(queries_t, grad)
        gq_block[b] = gq_sum.astype(GQ)
        gws = jnp.sum(gw_sum, axis=1, keepdims=True)
        gw_block[b] = dot(gather, jnp.where(l128 == hl * 4 + v128 % 4, gws, 0.0), HIGHEST)
        gkb[b] = gkt[:, b * BLK : b * BLK + BLK].T.reshape(4, 2, 2, 16, 128)
        remote(gkb.at[b, :, :, p.c[1]], rc.at[b], cs.at[b], cr.at[b], (0, 0, 0, 1)).start()
        if b % 2 == 1 and b < 7:
            reduce_x((b + 1) // 2)
            if b < 5:
                finish_x((b + 3) // 2)

    for h in range(8):
        gq[h] = gq_block[order_ref[h]].reshape(32, 4, 128)
    for g in range(4):
        total = gw_block[order_ref[2 * g]] + gw_block[order_ref[2 * g + 1]]
        gw[g] = total.reshape(32, 1, 128)
    reduce_x(0)

    def returned(o):
        heads, group = p.at(o)
        back = (4 - o[2]) % 4
        slot = (back % 2) * 16 + p.y8[o[1]] // 2 + p.x_low[o[0]] * 2 + back // 2
        remote(gq.at[pl.ds(group * 2, 2), slot], gq_out.at[:, p.flat], bs, br, o).start()
        remote(gw.at[group, slot], gw_recv.at[p.flat], us, ur, o).start()

    pltpu.make_async_copy(gq.at[mine, base], gq_out.at[:, p.flat], br).start()
    pltpu.make_async_copy(gw.at[p.group, base], gw_recv.at[p.flat], ur).start()
    finish_x(1)
    for o in ORDER:
        returned(o)
    finish_x(0)
    pltpu.make_async_copy(gw_recv, gw_recv, ur).wait()
    table = gw_recv[...].reshape(128, 128)
    lines = [[None] * 2 for _ in range(2)]
    for i in range(2):
        choose = one_hot(iota((128, 256), 1) == iota((128, 256), 0) * 2 + i)
        part = lax.dot_general(
            table, choose, (((0,), (0,)), ((), ())), precision=HIGHEST, preferred_element_type=F32
        )
        for hl in range(2):
            at = hl * 4 + i * 2
            lines[hl][i] = part[at : at + 2]
    for hl in range(2):
        gw_out[:, hl * 256 : hl * 256 + 256] = lines[hl][0] + lines[hl][1]
    for y in range(4):
        plane_each(y, lambda cp: cp.wait_send())
    total = v2[p.y[0], p.z[0]]
    for dy in range(4):
        for dz in range(4):
            if dy or dz:
                slot = p.y[dy] * 4 + p.z[dz]
                ref = rv.at[slot]
                pltpu.make_async_copy(ref, ref, vr.at[slot]).wait()
                total = total + rv[slot]
    gk_out[...] = total
    pltpu.make_async_copy(gq_out, gq_out, br).wait()
    for ref, sem in ((packed, qs), (gq_out, bs)):
        part = ref.at[:, pl.ds(0, 127)]
        pltpu.make_async_copy(part, part, sem).wait()
    for ref, sem in ((wsend, ws), (gw_recv, us)):
        part = ref.at[pl.ds(0, 127)]
        pltpu.make_async_copy(part, part, sem).wait()


GQ = BF16


def fused(*args):
    any_spec = pl.BlockSpec(memory_space=pl.ANY)
    vmem = pl.BlockSpec(memory_space=pltpu.VMEM)
    sem = pltpu.SemaphoreType.DMA
    return pl.pallas_call(
        fused_kernel,
        in_specs=[pl.BlockSpec(memory_space=pltpu.SMEM)] + [any_spec] * 6,
        out_specs=(any_spec, vmem, vmem),
        out_shape=(
            jax.ShapeDtypeStruct((2, 128, 4, 128), GQ),
            jax.ShapeDtypeStruct((2, 512), F32),
            jax.ShapeDtypeStruct((16, 128), F32),
        ),
        scratch_shapes=[
            pltpu.VMEM((4, 576, 512), BF16),
            pltpu.VMEM((1024, 128), BF16),
            pltpu.VMEM((2, 512), F32),
            pltpu.VMEM((1, 512), F32),
            pltpu.VMEM((16, 576), BF16),
            pltpu.VMEM((16, 128), BF16),
            pltpu.VMEM((512, 768), BF16),
            pltpu.VMEM((2, 128, 8, 640), BF16),
            pltpu.VMEM((128, 1, 128), F32),
            pltpu.VMEM((128, 1, 128), F32),
            pltpu.VMEM((8, 16, 8, 640), BF16),
            pltpu.VMEM((8, 16, 8, 640), BF16),
            pltpu.VMEM((4, 32, 1, 128), F32),
            pltpu.VMEM((3, 4, 2, 4, 2, 2, 16, 256), BF16),
            pltpu.VMEM((2, 128, 2048), F32),
            pltpu.VMEM((8, 128, 2048), F32),
            pltpu.VMEM((8, 8, 2048), F32),
            pltpu.VMEM((8, 8, 2048), F32),
            pltpu.VMEM((128, 2048), F32),
            pltpu.VMEM((8, 128, 128), GQ),
            pltpu.VMEM((8, 32, 128), F32),
            pltpu.VMEM((8, 32, 4, 128), GQ),
            pltpu.VMEM((4, 32, 1, 128), F32),
            pltpu.VMEM((8, 4, 2, 2, 16, 128), F32),
            pltpu.VMEM((8, 4, 2, 16, 128), F32),
            pltpu.VMEM((4, 4, 4, 16, 128), F32),
            pltpu.VMEM((4, 3, 4, 16, 128), F32),
            pltpu.VMEM((4, 4, 16, 128), F32),
            pltpu.VMEM((16, 16, 128), F32),
            sem((9,)),
            sem,
            sem((2,)),
            sem,
            sem,
            sem,
            sem((4, 9)),
            sem((4, 9)),
            sem((3, 4)),
            sem((3, 4)),
            sem((8,)),
            sem((8,)),
            sem((4, 3)),
            sem((4, 3)),
            sem((4, 4)),
            sem((16,)),
            sem,
            sem,
            sem,
            sem,
        ],
        compiler_params=pltpu.CompilerParams(
            has_side_effects=True, collective_id=1, vmem_limit_bytes=56 * 1024 * 1024
        ),
        name="fused",
    )(*args)


def on_device(q_main, latent, q_index, head_weight, k_index, token_weight, block_order):
    gq, gw, gk = fused(
        block_order,
        jnp.transpose(q_main, (1, 2, 0)),
        q_index.reshape(1024, 128),
        head_weight,
        token_weight.reshape(1, 512),
        latent,
        k_index,
    )
    return gq.astype(F32).reshape(512, 2, 128), gw, gk


def solution(mesh):
    return jax.shard_map(
        on_device,
        mesh=mesh,
        in_specs=(
            P("qgrp", "heads", None),
            P(("heads", "qgrp"), None),
            P("qgrp", "heads", None),
            P("heads", "qgrp"),
            P(("heads", "qgrp"), None),
            P("qgrp"),
            P(),
        ),
        out_specs=(P("qgrp", "heads", None), P("heads", "qgrp"), P(("heads", "qgrp"), None)),
        check_vma=False,
    )
```

```python
import math
import random

import jax
import jax.numpy as jnp
from jax import lax
from jax.experimental import pallas as pl
from jax.experimental.pallas import tpu as pltpu
from jax.sharding import PartitionSpec as P

MESH = pl.DeviceIdType.MESH
SCALE_INDEX = 128.0 ** (-0.5)
EXP_SCALE = 192.0 ** (-0.5) * math.log2(math.e)
NEG = -3.0e38
BLK = 256
F32 = jnp.float32
BF16 = jnp.bfloat16
HIGHEST = lax.Precision.HIGHEST


def far_first():
    every = [(a, b, c, d) for a in range(4) for b in range(4) for c in range(4) for d in range(2)][1:]
    random.Random(1).shuffle(every)
    return sorted(every, key=lambda o: sum(min(v, 4 - v) for v in o[:3]) + o[3] * 0.5)[::-1]


ORDER = far_first()
KEY_CUTS = (0, 16, 40, 80, 127)


class Place:
    def __init__(self):
        h = lax.axis_index("heads")
        q = lax.axis_index("qgrp")
        self.y = [lax.rem(lax.div(h, 8) + k, 4) for k in range(4)]
        self.z = [lax.rem(lax.rem(h, 4) + k, 4) for k in range(4)]
        x = lax.div(q, 2) * 2 + lax.rem(lax.div(h, 4), 2)
        self.x = [lax.rem(x + k, 4) for k in range(4)]
        self.c = [lax.rem(q, 2), 1 - lax.rem(q, 2)]
        self.x_low = [lax.rem(v, 2) for v in self.x]
        self.x_high = [lax.div(v, 2) for v in self.x]
        self.y8 = [v * 8 for v in self.y]
        self.xl4 = [v * 4 for v in self.x_low]
        self.xh2 = [v * 2 for v in self.x_high]
        self.heads, self.group = self.at((0, 0, 0, 0))
        self.flat = self.heads * 4 + self.group

    def at(self, o):
        dx, dy, dz, dc = o
        return self.y8[dy] + self.xl4[dx] + self.z[dz], self.xh2[dx] + self.c[dc]


def dev(heads, group):
    return {"heads": heads, "qgrp": group}


def enter(place):
    sem = pltpu.get_barrier_semaphore()
    for o in ORDER:
        pl.semaphore_signal(sem, inc=1, device_id=dev(*place.at(o)), device_id_type=MESH)
    return sem


def iota(shape, dim):
    return lax.broadcasted_iota(jnp.int32, shape, dim)


def dot_t(a, b, precision=None):
    return lax.dot_general(
        a, b, (((1,), (1,)), ((), ())), precision=precision, preferred_element_type=F32
    )


def dot(a, b, precision=None):
    return jnp.dot(a, b, precision=precision, preferred_element_type=F32)


def one_hot(mask):
    return jnp.where(mask, 1.0, 0.0)


PARTS = ((0, 2), (1, 3))


def fused_kernel(
    order_ref,
    main_hbm,
    index_hbm,
    weight_hbm,
    token_hbm,
    latent_hbm,
    key_hbm,
    gq_out,
    gw_out,
    gk_out,
    main,
    index,
    weight,
    token_in,
    latent,
    key,
    perm,
    packed,
    wsend,
    gw_recv,
    recv0,
    recv1,
    wrecv,
    keys,
    s_buf,
    r_buf,
    t_buf,
    l_buf,
    gkt,
    gq_block,
    gw_block,
    gq,
    gw,
    gkb,
    rc,
    v1,
    rx,
    v2,
    rv,
    ms,
    qs,
    qr,
    ws,
    wr,
    ls,
    ags,
    agr,
    fs,
    fr,
    cs,
    cr,
    xs,
    xr,
    vs,
    vr,
    bs,
    br,
    us,
    ur,
):
    p = Place()
    tiles = [
        pltpu.make_async_copy(
            main_hbm.at[:, :, pl.ds(t * 128, 128)], main.at[:, :, pl.ds(t * 128, 128)], ms.at[t]
        )
        for t in range(4)
    ]
    small = [
        pltpu.make_async_copy(src, dst, ms.at[4 + at])
        for at, (src, dst) in enumerate(
            (
                (latent_hbm, latent),
                (key_hbm, key),
                (index_hbm, index),
                (weight_hbm, weight),
                (token_hbm, token_in),
            )
        )
    ]
    for cp in small[0:2] + tiles + small[2:]:
        cp.start()
    barrier = enter(p)
    recv = (recv0, recv1)
    mine = pl.ds(p.group * 2, 2)
    base = p.y[0] * 4 + p.x_low[0] * 2

    def remote(src, dst, ssem, rsem, o):
        return pltpu.make_async_remote_copy(
            src_ref=src,
            dst_ref=dst,
            send_sem=ssem,
            recv_sem=rsem,
            device_id=dev(*p.at(o)),
            device_id_type=MESH,
        )

    def key_phase(number):
        copies = []
        for color, axes in enumerate(("zyx", "yxz", "xzy")):
            done = axes[:number]
            ref = keys.at[
                color,
                slice(None) if "y" in done else p.y[0],
                slice(None) if "x" in done else p.x_low[0],
                slice(None) if "z" in done else p.z[0],
                slice(None) if "x" in done else p.x_high[0],
                p.c[0],
            ]
            for j in range(1, 4):
                o = tuple(j if axis == axes[number] else 0 for axis in "xyz") + (0,)
                at = color * 3 + j - 1
                copies.append(remote(ref, ref, ags.at[number, at], agr.at[number, at], o))
        return copies

    def to_partner(number, at, ref):
        return remote(ref, ref, fs.at[number, at], fr.at[number, at], (0, 0, 0, 1))

    def block(color, axes, number, o):
        done = axes[:number]
        return keys.at[
            color,
            slice(None) if "y" in done else p.y[-o[1] % 4],
            slice(None) if "x" in done else p.x_low[-o[0] % 4],
            slice(None) if "z" in done else p.z[-o[2] % 4],
            slice(None) if "x" in done else p.x_high[-o[0] % 4],
            p.c[0],
        ]

    def sent(count, at):
        part = packed.at[:, pl.ds(0, count)]
        pltpu.make_async_copy(part, part, qs.at[at]).wait()

    def send(o, at):
        heads, group = p.at(o)
        e = heads * 4 + group
        part, slot = o[2] % 2, o[2] // 2
        remote(packed.at[:, e], recv[part].at[mine, base + slot], qs.at[at], qr.at[part], o).start()
        remote(wsend.at[e], wrecv.at[p.group, part * 16 + base + slot], ws, wr, o).start()

    def pack_tile(t):
        lanes = pl.ds(t * 128, 128)
        both = jnp.concatenate([main[h, :, lanes] for h in range(4)], axis=1)
        rows = dot_t(perm[:, 0:512], both)
        tail = dot(perm[:, 512:768], index[t * 256 : t * 256 + 256])
        lane, row = iota((512, 128), 1), iota((512, 128), 0)
        tail = jnp.where(row % 2 == 0, pltpu.roll(tail, 64, 1), tail)
        last = jnp.concatenate([rows[:, 512:576], jnp.zeros((512, 64), F32)], axis=1)
        last = jnp.where(lane < 64, last, tail)
        full = jnp.concatenate([rows[:, 0:512], last], axis=1).astype(BF16)
        packed[t // 2, (t % 2) * 64 : (t % 2) * 64 + 64] = full.reshape(64, 8, 640)

    def pack_weights():
        total = jnp.zeros((128, 128), F32)
        sub = iota((128, 256), 0)
        for hl in range(2):
            cols = slice(hl * 256, hl * 256 + 256)
            for i in range(2):
                table = jnp.zeros((128, 256), F32)
                for at, line in (
                    (hl * 4 + i * 2, weight[0:1, cols]),
                    (hl * 4 + i * 2 + 1, weight[1:2, cols]),
                    (8 + hl * 2 + i, token_in[0:1, cols]),
                ):
                    table = jnp.where(sub == at, jnp.broadcast_to(line, (128, 256)), table)
                choose = one_hot(iota((128, 256), 1) == iota((128, 256), 0) * 2 + i)
                total = total + dot_t(choose, table, HIGHEST)
        wsend[...] = total.reshape(128, 1, 128)

    small[0].wait()
    small[1].wait()
    at = (p.y[0], p.x_low[0], p.z[0], p.x_high[0], p.c[0])
    keys[(0,) + at] = latent[:, 0:256]
    keys[(1,) + at] = latent[:, 256:512]
    keys[(2,) + at] = jnp.concatenate([latent[:, 512:576], jnp.zeros((16, 64), BF16), key[...]], axis=1)
    out, src = iota((512, 512), 0), iota((512, 512), 1)
    perm[:, 0:512] = one_hot(out == (src % 128) * 4 + src // 128).astype(BF16)
    out, src = iota((512, 256), 0), iota((512, 256), 1)
    perm[:, 512:768] = one_hot(src == out // 2).astype(BF16)
    pl.semaphore_wait(barrier, 127)
    order = [o for part in PARTS for o in ORDER if o[2] in part]
    colors = list(enumerate(("zyx", "yxz", "xzy")))
    forwards = []
    for number in range(3):
        phase = key_phase(number)
        for cp in phase:
            cp.start()
        if number == 0:
            for cp in small[2:]:
                cp.wait()
            pack_weights()
            for t in range(4):
                tiles[t].wait()
                pack_tile(t)
        elif number == 1:
            pltpu.make_async_copy(packed.at[:, p.flat], recv0.at[mine, base], qr.at[0]).start()
            pltpu.make_async_copy(wsend.at[p.flat], wrecv.at[p.group, base], wr).start()
            for at, o in enumerate(order[0:63]):
                send(o, at // EARLY)
        else:
            for color, axes in colors:
                cp = to_partner(color, 0, block(color, axes, 2, (0, 0, 0, 0)))
                cp.start()
                forwards.append(cp)
            sent(EARLY, 0)
            for o in order[63:127]:
                send(o, 2)
        for j in range(1, 4):
            for color, axes in colors:
                phase[color * 3 + j - 1].wait()
                if number == 2:
                    o = tuple(j if axis == axes[2] else 0 for axis in "xyz")
                    cp = to_partner(color, j, block(color, axes, 2, o))
                    cp.start()
                    forwards.append(cp)
    for cp in forwards:
        cp.wait()

    e2 = p.flat * 2
    spread = one_hot(iota((64, 16), 1) == iota((64, 16), 0) // 4)
    gather = one_hot(iota((32, 128), 1) // 4 == iota((32, 128), 0))
    even = one_hot(iota((64, 128), 1) == iota((64, 128), 0) * 2).astype(BF16)
    odd = one_hot(iota((64, 128), 1) == iota((64, 128), 0) * 2 + 1).astype(BF16)
    f_out, f_in = iota((8, 8), 0), iota((8, 8), 1)
    fold_t = one_hot(f_in // 4 == (f_out // 2) % 2)
    fold_l = one_hot((f_in // 2) % 2 == (f_out // 2) % 2)
    l64, v64 = iota((64, 128), 1), iota((64, 128), 0)
    l128, v128 = iota((128, 128), 1), iota((128, 128), 0)
    row8, lane8 = (iota((8, 128), 0) // 2) % 2, iota((8, 128), 1)

    def half_of(b):
        h = 0
        for at in range(1, 8):
            h = jnp.where(order_ref[at] == b, at, h)
        return h, lax.div(h, 2), lax.rem(h, 2)

    def index_queries(part, h):
        tail = recv[part][h, :, :, 512:640].reshape(128, 128)
        low = pltpu.roll(dot(even, tail), 64, 1)
        return jnp.where(l64 < 64, low, dot(odd, tail)).astype(BF16)

    def weight_column(part, g, hl):
        table = dot(spread, wrecv[g, pl.ds(part * 16, 16), 0, :], HIGHEST)
        return jnp.sum(jnp.where(l64 == hl * 4 + v64 % 4, table, 0.0), axis=1, keepdims=True)

    def key_block(kb):
        parts = [keys[color, kb // 2, kb % 2].reshape(256, 256) for color in range(3)]
        return jnp.concatenate(parts, axis=1)

    def forward(part):
        for b in range(7, -1, -1):
            n = (b + 1) * BLK
            par = b % 2
            h, g, hl = half_of(b)
            x = recv[part][h].reshape(128, 640)
            for kb in range(b + 1):
                cols = slice(kb * BLK, kb * BLK + BLK)
                s = dot_t(x, key_block(kb)[:, 0:640])
                if kb == b:
                    row = (iota((128, BLK), 0) % 8) // 4
                    s = jnp.where(iota((128, BLK), 1) - row <= e2, s, NEG)
                s_buf[par, :, cols] = s

            def softmax_rows(r):
                rows = slice(r * 32, r * 32 + 32)
                s = s_buf[par, rows, 0:n]
                top = jnp.max(s, axis=1, keepdims=True)
                w = jnp.exp2((s - top) * EXP_SCALE)
                inv = (1.0 / 128.0) / jnp.sum(w, axis=1, keepdims=True)
                add = jnp.sum((w * inv).reshape(4, 8, n), axis=0)
                if part == 0 and r == 0:
                    t_buf[b, :, 0:n] = add
                else:
                    t_buf[b, :, 0:n] += add

            for r in range(4):
                softmax_rows(r)

            queries = index_queries(part, h)
            wcol = weight_column(part, g, hl)
            for kb in range(b + 1):
                cols = slice(kb * BLK, kb * BLK + BLK)
                relu = jnp.maximum(dot_t(queries, key_block(kb)[:, 640:768]) * SCALE_INDEX, 0.0)
                r_buf[b, part * 64 : part * 64 + 64, cols] = relu
                add = jnp.sum((relu * wcol).reshape(8, 8, BLK), axis=0)
                if part == 0:
                    l_buf[b, :, cols] = add
                else:
                    l_buf[b, :, cols] += add

    def reduce_x(y):
        for b in (2 * y + 1, 2 * y):
            cp = remote(gkb.at[b, :, :, p.c[1]], rc.at[b], cs.at[b], cr.at[b], (0, 0, 0, 1))
            cp.wait()
        for x in range(4):
            b = 2 * y + x % 2
            v1[y, x] = (gkb[b, :, x // 2, p.c[0]] + rc[b, :, x // 2]).astype(BF16)
        own = 2 * y + p.x_low[0]
        v2[y] = gkb[own, :, p.x_high[0], p.c[0]] + rc[own, :, p.x_high[0]]
        for cp in x_copies(y):
            cp.start()

    def x_copies(y):
        return [
            remote(v1.at[y, p.x[j]], rx.at[y, j - 1], xs.at[y, j - 1], xr.at[y, j - 1], (j, 0, 0, 0))
            for j in range(1, 4)
        ]

    def plane_copy(y, j):
        slot = p.y[0] * 4 + p.z[0]
        return pltpu.make_async_remote_copy(
            src_ref=v2.at[y, p.z[j]],
            dst_ref=rv.at[slot],
            send_sem=vs.at[y, j],
            recv_sem=vr.at[slot],
            device_id=dev(y * 8 + p.xl4[0] + p.z[j], p.group),
            device_id_type=MESH,
        )

    def plane_each(y, action):
        for j in range(4):
            if j:
                action(plane_copy(y, j))
            else:

                @pl.when(p.y[0] != y)
                def _():
                    action(plane_copy(y, 0))

    def finish_x(y):
        for cp in x_copies(y):
            cp.wait()
        v2[y] = v2[y] + rx[y, 0].astype(F32) + rx[y, 1].astype(F32) + rx[y, 2].astype(F32)
        plane_each(y, lambda cp: cp.start())

    pltpu.make_async_copy(recv0, recv0, qr.at[0]).wait()
    pltpu.make_async_copy(wrecv, wrecv, wr).wait()
    forward(0)
    pltpu.make_async_copy(recv1, recv1, qr.at[1]).wait()
    forward(1)

    gkt[...] = jnp.zeros_like(gkt)
    for b in range(7, -1, -1):
        n = (b + 1) * BLK
        h, g, hl = half_of(b)
        target = dot(fold_t, t_buf[b, :, 0:n], HIGHEST)
        logits = dot(fold_l, l_buf[b, :, 0:n], HIGHEST)
        visible = iota((8, n), 1) - (iota((8, n), 0) // 2) % 2 <= e2 + b * BLK
        logits = jnp.where(visible, logits, NEG)
        top = jnp.max(logits, axis=1, keepdims=True)
        expo = jnp.exp(logits - top)
        probs = expo / jnp.sum(expo, axis=1, keepdims=True)
        token = jnp.broadcast_to(wrecv[g, 0], (8, 128))
        token = jnp.sum(jnp.where(lane8 == 8 + hl * 2 + row8, token, 0.0), axis=1, keepdims=True)
        l_buf[b, :, 0:n] = token * (probs - target)

        queries = jnp.concatenate([index_queries(part, h) for part in range(2)], axis=0)
        wcol = jnp.concatenate([weight_column(part, g, hl) for part in range(2)], axis=0)
        queries_t = queries.T
        wscaled = wcol * SCALE_INDEX
        gq_sum = jnp.zeros((128, 128), F32)
        gw_sum = jnp.zeros((128, 128), F32)
        for kb in range(b + 1):
            cols = slice(kb * BLK, kb * BLK + BLK)
            relu = r_buf[b, :, cols]
            dl = jnp.broadcast_to(l_buf[b, :, cols][None], (16, 8, BLK)).reshape(128, BLK)
            gwp = dl * relu
            gw_sum = gw_sum + gwp[:, 0:128] + gwp[:, 128:256]
            grad = jnp.where(relu > 0.0, dl * wscaled, 0.0).astype(BF16)
            gq_sum = gq_sum + dot(grad, key_block(kb)[:, 640:768])
            gkt[:, cols] += dot(queries_t, grad)
        gq_block[b] = gq_sum.astype(GQ)
        gws = jnp.sum(gw_sum, axis=1, keepdims=True)
        gw_block[b] = dot(gather, jnp.where(l128 == hl * 4 + v128 % 4, gws, 0.0), HIGHEST)
        gkb[b] = gkt[:, b * BLK : b * BLK + BLK].T.reshape(4, 2, 2, 16, 128)
        remote(gkb.at[b, :, :, p.c[1]], rc.at[b], cs.at[b], cr.at[b], (0, 0, 0, 1)).start()
        if b % 2 == 1 and b < 7:
            reduce_x((b + 1) // 2)
            if b < 5:
                finish_x((b + 3) // 2)

    for h in range(8):
        gq[h] = gq_block[order_ref[h]].reshape(32, 4, 128)
    for g in range(4):
        total = gw_block[order_ref[2 * g]] + gw_block[order_ref[2 * g + 1]]
        gw[g] = total.reshape(32, 1, 128)
    def returned(o):
        heads, group = p.at(o)
        back = (4 - o[2]) % 4
        slot = (back % 2) * 16 + p.y8[o[1]] // 2 + p.x_low[o[0]] * 2 + back // 2
        remote(gq.at[pl.ds(group * 2, 2), slot], gq_out.at[:, p.flat], bs, br, o).start()
        remote(gw.at[group, slot], gw_recv.at[p.flat], us, ur, o).start()

    pltpu.make_async_copy(gq.at[mine, base], gq_out.at[:, p.flat], br).start()
    pltpu.make_async_copy(gw.at[p.group, base], gw_recv.at[p.flat], ur).start()
    for o in ORDER[0:30]:
        returned(o)
    reduce_x(0)
    finish_x(1)
    for o in ORDER[30:127]:
        returned(o)
    finish_x(0)
    pltpu.make_async_copy(gw_recv, gw_recv, ur).wait()
    table = gw_recv[...].reshape(128, 128)
    lines = [[None] * 2 for _ in range(2)]
    for i in range(2):
        choose = one_hot(iota((128, 256), 1) == iota((128, 256), 0) * 2 + i)
        part = lax.dot_general(
            table, choose, (((0,), (0,)), ((), ())), precision=HIGHEST, preferred_element_type=F32
        )
        for hl in range(2):
            at = hl * 4 + i * 2
            lines[hl][i] = part[at : at + 2]
    for hl in range(2):
        gw_out[:, hl * 256 : hl * 256 + 256] = lines[hl][0] + lines[hl][1]
    for y in range(4):
        plane_each(y, lambda cp: cp.wait_send())
    total = v2[p.y[0], p.z[0]]
    for dy in range(4):
        for dz in range(4):
            if dy or dz:
                slot = p.y[dy] * 4 + p.z[dz]
                ref = rv.at[slot]
                pltpu.make_async_copy(ref, ref, vr.at[slot]).wait()
                total = total + rv[slot]
    gk_out[...] = total
    pltpu.make_async_copy(gq_out, gq_out, br).wait()
    sent(63 - EARLY, 1)
    sent(64, 2)
    part = gq_out.at[:, pl.ds(0, 127)]
    pltpu.make_async_copy(part, part, bs).wait()
    for ref, sem in ((wsend, ws), (gw_recv, us)):
        part = ref.at[pl.ds(0, 127)]
        pltpu.make_async_copy(part, part, sem).wait()


GQ = BF16
EARLY = 46


def fused(*args):
    any_spec = pl.BlockSpec(memory_space=pl.ANY)
    vmem = pl.BlockSpec(memory_space=pltpu.VMEM)
    sem = pltpu.SemaphoreType.DMA
    return pl.pallas_call(
        fused_kernel,
        in_specs=[pl.BlockSpec(memory_space=pltpu.SMEM)] + [any_spec] * 6,
        out_specs=(any_spec, vmem, vmem),
        out_shape=(
            jax.ShapeDtypeStruct((2, 128, 4, 128), GQ),
            jax.ShapeDtypeStruct((2, 512), F32),
            jax.ShapeDtypeStruct((16, 128), F32),
        ),
        scratch_shapes=[
            pltpu.VMEM((4, 576, 512), BF16),
            pltpu.VMEM((1024, 128), BF16),
            pltpu.VMEM((2, 512), F32),
            pltpu.VMEM((1, 512), F32),
            pltpu.VMEM((16, 576), BF16),
            pltpu.VMEM((16, 128), BF16),
            pltpu.VMEM((512, 768), BF16),
            pltpu.VMEM((2, 128, 8, 640), BF16),
            pltpu.VMEM((128, 1, 128), F32),
            pltpu.VMEM((128, 1, 128), F32),
            pltpu.VMEM((8, 16, 8, 640), BF16),
            pltpu.VMEM((8, 16, 8, 640), BF16),
            pltpu.VMEM((4, 32, 1, 128), F32),
            pltpu.VMEM((3, 4, 2, 4, 2, 2, 16, 256), BF16),
            pltpu.VMEM((2, 128, 2048), F32),
            pltpu.VMEM((8, 128, 2048), F32),
            pltpu.VMEM((8, 8, 2048), F32),
            pltpu.VMEM((8, 8, 2048), F32),
            pltpu.VMEM((128, 2048), F32),
            pltpu.VMEM((8, 128, 128), GQ),
            pltpu.VMEM((8, 32, 128), F32),
            pltpu.VMEM((8, 32, 4, 128), GQ),
            pltpu.VMEM((4, 32, 1, 128), F32),
            pltpu.VMEM((8, 4, 2, 2, 16, 128), F32),
            pltpu.VMEM((8, 4, 2, 16, 128), F32),
            pltpu.VMEM((4, 4, 4, 16, 128), BF16),
            pltpu.VMEM((4, 3, 4, 16, 128), BF16),
            pltpu.VMEM((4, 4, 16, 128), F32),
            pltpu.VMEM((16, 16, 128), F32),
            sem((9,)),
            sem((3,)),
            sem((2,)),
            sem,
            sem,
            sem,
            sem((4, 9)),
            sem((4, 9)),
            sem((3, 4)),
            sem((3, 4)),
            sem((8,)),
            sem((8,)),
            sem((4, 3)),
            sem((4, 3)),
            sem((4, 4)),
            sem((16,)),
            sem,
            sem,
            sem,
            sem,
        ],
        compiler_params=pltpu.CompilerParams(
            has_side_effects=True, collective_id=1, vmem_limit_bytes=56 * 1024 * 1024
        ),
        name="fused",
    )(*args)


def finish_kernel(gq, gw, gk, gq_out, gw_out, gk_out):
    gq_out[...] = gq[...].astype(F32)
    gw_out[...] = gw[...]
    gk_out[...] = gk[...]


def finish(gq, gw, gk):
    return pl.pallas_call(
        finish_kernel,
        grid=(2,),
        in_specs=[
            pl.BlockSpec((512, 128), lambda t: (t, 0)),
            pl.BlockSpec((2, 512), lambda t: (0, 0)),
            pl.BlockSpec((16, 128), lambda t: (0, 0)),
        ],
        out_specs=(
            pl.BlockSpec((512, 128), lambda t: (t, 0)),
            pl.BlockSpec((2, 512), lambda t: (0, 0)),
            pl.BlockSpec((16, 128), lambda t: (0, 0)),
        ),
        out_shape=(
            jax.ShapeDtypeStruct((1024, 128), F32),
            jax.ShapeDtypeStruct((2, 512), F32),
            jax.ShapeDtypeStruct((16, 128), F32),
        ),
        name="finish",
    )(gq, gw, gk)


def on_device(q_main, latent, q_index, head_weight, k_index, token_weight, block_order):
    gq, gw, gk = fused(
        block_order,
        jnp.transpose(q_main, (1, 2, 0)),
        q_index.reshape(1024, 128),
        head_weight,
        token_weight.reshape(1, 512),
        latent,
        k_index,
    )
    gq, gw, gk = finish(gq.reshape(1024, 128), gw, gk)
    return gq.reshape(512, 2, 128), gw, gk


def solution(mesh):
    return jax.shard_map(
        on_device,
        mesh=mesh,
        in_specs=(
            P("qgrp", "heads", None),
            P(("heads", "qgrp"), None),
            P("qgrp", "heads", None),
            P("heads", "qgrp"),
            P(("heads", "qgrp"), None),
            P("qgrp"),
            P(),
        ),
        out_specs=(P("qgrp", "heads", None), P("heads", "qgrp"), P(("heads", "qgrp"), None)),
        check_vma=False,
    )
```

```python
import math
import random

import jax
import jax.numpy as jnp
from jax import lax
from jax.experimental import pallas as pl
from jax.experimental.pallas import tpu as pltpu
from jax.sharding import PartitionSpec as P

MESH = pl.DeviceIdType.MESH
SCALE_INDEX = 128.0 ** (-0.5)
EXP_SCALE = 192.0 ** (-0.5) * math.log2(math.e)
NEG = -3.0e38
BLK = 256
F32 = jnp.float32
BF16 = jnp.bfloat16
HIGHEST = lax.Precision.HIGHEST


def far_first():
    every = [(a, b, c, d) for a in range(4) for b in range(4) for c in range(4) for d in range(2)][1:]
    random.Random(1).shuffle(every)
    return sorted(every, key=lambda o: sum(min(v, 4 - v) for v in o[:3]) + o[3] * 0.5)[::-1]


ORDER = far_first()
KEY_CUTS = (0, 16, 40, 80, 127)


class Place:
    def __init__(self):
        h = lax.axis_index("heads")
        q = lax.axis_index("qgrp")
        self.y = [lax.rem(lax.div(h, 8) + k, 4) for k in range(4)]
        self.z = [lax.rem(lax.rem(h, 4) + k, 4) for k in range(4)]
        x = lax.div(q, 2) * 2 + lax.rem(lax.div(h, 4), 2)
        self.x = [lax.rem(x + k, 4) for k in range(4)]
        self.c = [lax.rem(q, 2), 1 - lax.rem(q, 2)]
        self.x_low = [lax.rem(v, 2) for v in self.x]
        self.x_high = [lax.div(v, 2) for v in self.x]
        self.y8 = [v * 8 for v in self.y]
        self.xl4 = [v * 4 for v in self.x_low]
        self.xh2 = [v * 2 for v in self.x_high]
        self.heads, self.group = self.at((0, 0, 0, 0))
        self.flat = self.heads * 4 + self.group

    def at(self, o):
        dx, dy, dz, dc = o
        return self.y8[dy] + self.xl4[dx] + self.z[dz], self.xh2[dx] + self.c[dc]


def dev(heads, group):
    return {"heads": heads, "qgrp": group}


def enter(place):
    sem = pltpu.get_barrier_semaphore()
    for o in ORDER:
        pl.semaphore_signal(sem, inc=1, device_id=dev(*place.at(o)), device_id_type=MESH)
    return sem


def iota(shape, dim):
    return lax.broadcasted_iota(jnp.int32, shape, dim)


def dot_t(a, b, precision=None):
    return lax.dot_general(
        a, b, (((1,), (1,)), ((), ())), precision=precision, preferred_element_type=F32
    )


def dot(a, b, precision=None):
    return jnp.dot(a, b, precision=precision, preferred_element_type=F32)


def one_hot(mask):
    return jnp.where(mask, 1.0, 0.0)


PARTS = ((0, 2), (1, 3))


def fused_kernel(
    order_ref,
    main_hbm,
    index_hbm,
    weight_hbm,
    token_hbm,
    latent_hbm,
    key_hbm,
    gq_out,
    gw_out,
    gk_out,
    main,
    index,
    weight,
    token_in,
    latent,
    key,
    perm,
    packed,
    wsend,
    gw_recv,
    recv0,
    recv1,
    wrecv0,
    wrecv1,
    keys,
    s_buf,
    r_buf,
    t_buf,
    l_buf,
    gkt,
    gq_block,
    gw_block,
    gq,
    gw,
    gkb,
    rc,
    v1,
    rx,
    v2,
    rv,
    ms,
    qs,
    qr,
    ws,
    wr,
    ls,
    ags,
    agr,
    fs,
    fr,
    cs,
    cr,
    xs,
    xr,
    vs,
    vr,
    bs,
    br,
    us,
    ur,
):
    p = Place()
    tiles = [
        pltpu.make_async_copy(
            main_hbm.at[:, :, pl.ds(t * 128, 128)], main.at[:, :, pl.ds(t * 128, 128)], ms.at[t]
        )
        for t in range(4)
    ]
    small = [
        pltpu.make_async_copy(src, dst, ms.at[4 + at])
        for at, (src, dst) in enumerate(
            (
                (latent_hbm, latent),
                (key_hbm, key),
                (index_hbm, index),
                (weight_hbm, weight),
                (token_hbm, token_in),
            )
        )
    ]
    for cp in small[0:2] + tiles + small[2:]:
        cp.start()
    barrier = enter(p)
    recv = (recv0, recv1)
    wrecv = (wrecv0, wrecv1)
    mine = pl.ds(p.group * 2, 2)
    base = p.y[0] * 4 + p.x_low[0] * 2

    def remote(src, dst, ssem, rsem, o):
        return pltpu.make_async_remote_copy(
            src_ref=src,
            dst_ref=dst,
            send_sem=ssem,
            recv_sem=rsem,
            device_id=dev(*p.at(o)),
            device_id_type=MESH,
        )

    def key_phase(number):
        copies = []
        for color, axes in enumerate(("zyx", "yxz", "xzy")):
            done = axes[:number]
            ref = keys.at[
                color,
                slice(None) if "y" in done else p.y[0],
                slice(None) if "x" in done else p.x_low[0],
                slice(None) if "z" in done else p.z[0],
                slice(None) if "x" in done else p.x_high[0],
                p.c[0],
            ]
            for j in range(1, 4):
                o = tuple(j if axis == axes[number] else 0 for axis in "xyz") + (0,)
                at = color * 3 + j - 1
                copies.append(remote(ref, ref, ags.at[number, at], agr.at[number, at], o))
        return copies

    def to_partner(number, at, ref):
        return remote(ref, ref, fs.at[number, at], fr.at[number, at], (0, 0, 0, 1))

    def block(color, axes, number, o):
        done = axes[:number]
        return keys.at[
            color,
            slice(None) if "y" in done else p.y[-o[1] % 4],
            slice(None) if "x" in done else p.x_low[-o[0] % 4],
            slice(None) if "z" in done else p.z[-o[2] % 4],
            slice(None) if "x" in done else p.x_high[-o[0] % 4],
            p.c[0],
        ]

    def sent(count, at):
        part = packed.at[:, pl.ds(0, count)]
        pltpu.make_async_copy(part, part, qs.at[at]).wait()

    def send(o, at):
        heads, group = p.at(o)
        e = heads * 4 + group
        part, slot = o[2] % 2, o[2] // 2
        remote(packed.at[:, e], recv[part].at[mine, base + slot], qs.at[at], qr.at[part], o).start()
        remote(wsend.at[e], wrecv[part].at[p.group, base + slot], ws, wr.at[part], o).start()

    def pack_tile(t):
        lanes = pl.ds(t * 128, 128)
        both = jnp.concatenate([main[h, :, lanes] for h in range(4)], axis=1)
        rows = dot_t(perm[:, 0:512], both)
        tail = dot(perm[:, 512:768], index[t * 256 : t * 256 + 256])
        lane, row = iota((512, 128), 1), iota((512, 128), 0)
        tail = jnp.where(row % 2 == 0, pltpu.roll(tail, 64, 1), tail)
        last = jnp.concatenate([rows[:, 512:576], jnp.zeros((512, 64), F32)], axis=1)
        last = jnp.where(lane < 64, last, tail)
        full = jnp.concatenate([rows[:, 0:512], last], axis=1).astype(BF16)
        packed[t // 2, (t % 2) * 64 : (t % 2) * 64 + 64] = full.reshape(64, 8, 640)

    def pack_weights():
        total = jnp.zeros((128, 128), F32)
        sub = iota((128, 256), 0)
        for hl in range(2):
            cols = slice(hl * 256, hl * 256 + 256)
            for i in range(2):
                table = jnp.zeros((128, 256), F32)
                for at, line in (
                    (hl * 4 + i * 2, weight[0:1, cols]),
                    (hl * 4 + i * 2 + 1, weight[1:2, cols]),
                    (8 + hl * 2 + i, token_in[0:1, cols]),
                ):
                    table = jnp.where(sub == at, jnp.broadcast_to(line, (128, 256)), table)
                choose = one_hot(iota((128, 256), 1) == iota((128, 256), 0) * 2 + i)
                total = total + dot_t(choose, table, HIGHEST)
        wsend[...] = total.reshape(128, 1, 128)

    small[0].wait()
    small[1].wait()
    at = (p.y[0], p.x_low[0], p.z[0], p.x_high[0], p.c[0])
    keys[(0,) + at] = latent[:, 0:256]
    keys[(1,) + at] = latent[:, 256:512]
    keys[(2,) + at] = jnp.concatenate([latent[:, 512:576], jnp.zeros((16, 64), BF16), key[...]], axis=1)
    out, src = iota((512, 512), 0), iota((512, 512), 1)
    perm[:, 0:512] = one_hot(out == (src % 128) * 4 + src // 128).astype(BF16)
    out, src = iota((512, 256), 0), iota((512, 256), 1)
    perm[:, 512:768] = one_hot(src == out // 2).astype(BF16)
    pl.semaphore_wait(barrier, 127)
    order = [o for part in PARTS for o in ORDER if o[2] in part]
    colors = list(enumerate(("zyx", "yxz", "xzy")))
    forwards = []
    for number in range(3):
        phase = key_phase(number)
        for cp in phase:
            cp.start()
        if number == 0:
            for cp in small[2:]:
                cp.wait()
            pack_weights()
            for t in range(4):
                tiles[t].wait()
                pack_tile(t)
        elif number == 1:
            pltpu.make_async_copy(packed.at[:, p.flat], recv0.at[mine, base], qr.at[0]).start()
            pltpu.make_async_copy(wsend.at[p.flat], wrecv0.at[p.group, base], wr.at[0]).start()
            for at, o in enumerate(order[0:FIRST]):
                send(o, at // EARLY)
        else:
            for color, axes in colors:
                cp = to_partner(color, 0, block(color, axes, 2, (0, 0, 0, 0)))
                cp.start()
                forwards.append(cp)
            for at, o in enumerate(order[FIRST:63], FIRST):
                send(o, at // EARLY)
            sent(EARLY, 0)
            for o in order[63:127]:
                send(o, 2)
        for j in range(1, 4):
            for color, axes in colors:
                phase[color * 3 + j - 1].wait()
                if number == 2:
                    o = tuple(j if axis == axes[2] else 0 for axis in "xyz")
                    cp = to_partner(color, j, block(color, axes, 2, o))
                    cp.start()
                    forwards.append(cp)
    for cp in forwards:
        cp.wait()

    e2 = p.flat * 2
    spread = one_hot(iota((64, 16), 1) == iota((64, 16), 0) // 4)
    gather = one_hot(iota((32, 128), 1) // 4 == iota((32, 128), 0))
    even = one_hot(iota((64, 128), 1) == iota((64, 128), 0) * 2).astype(BF16)
    odd = one_hot(iota((64, 128), 1) == iota((64, 128), 0) * 2 + 1).astype(BF16)
    f_out, f_in = iota((8, 8), 0), iota((8, 8), 1)
    fold_t = one_hot(f_in // 4 == (f_out // 2) % 2)
    fold_l = one_hot((f_in // 2) % 2 == (f_out // 2) % 2)
    l64, v64 = iota((64, 128), 1), iota((64, 128), 0)
    l128, v128 = iota((128, 128), 1), iota((128, 128), 0)
    row8, lane8 = (iota((8, 128), 0) // 2) % 2, iota((8, 128), 1)

    def half_of(b):
        h = 0
        for at in range(1, 8):
            h = jnp.where(order_ref[at] == b, at, h)
        return h, lax.div(h, 2), lax.rem(h, 2)

    def index_queries(part, h):
        tail = recv[part][h, :, :, 512:640].reshape(128, 128)
        low = pltpu.roll(dot(even, tail), 64, 1)
        return jnp.where(l64 < 64, low, dot(odd, tail)).astype(BF16)

    def weight_column(part, g, hl):
        table = dot(spread, wrecv[part][g, :, 0, :], HIGHEST)
        return jnp.sum(jnp.where(l64 == hl * 4 + v64 % 4, table, 0.0), axis=1, keepdims=True)

    def key_block(kb):
        parts = [keys[color, kb // 2, kb % 2].reshape(256, 256) for color in range(3)]
        return jnp.concatenate(parts, axis=1)

    def forward(part):
        for b in range(7, -1, -1):
            n = (b + 1) * BLK
            par = b % 2
            h, g, hl = half_of(b)
            x = recv[part][h].reshape(128, 640)
            for kb in range(b + 1):
                cols = slice(kb * BLK, kb * BLK + BLK)
                s = dot_t(x, key_block(kb)[:, 0:640])
                if kb == b:
                    row = (iota((128, BLK), 0) % 8) // 4
                    s = jnp.where(iota((128, BLK), 1) - row <= e2, s, NEG)
                s_buf[par, :, cols] = s

            def softmax_rows(r):
                rows = slice(r * 32, r * 32 + 32)
                s = s_buf[par, rows, 0:n]
                top = jnp.max(s, axis=1, keepdims=True)
                w = jnp.exp2((s - top) * EXP_SCALE)
                inv = (1.0 / 128.0) / jnp.sum(w, axis=1, keepdims=True)
                add = jnp.sum((w * inv).reshape(4, 8, n), axis=0)
                if part == 0 and r == 0:
                    t_buf[b, :, 0:n] = add
                else:
                    t_buf[b, :, 0:n] += add

            for r in range(4):
                softmax_rows(r)

            queries = index_queries(part, h)
            wcol = weight_column(part, g, hl)
            for kb in range(b + 1):
                cols = slice(kb * BLK, kb * BLK + BLK)
                relu = jnp.maximum(dot_t(queries, key_block(kb)[:, 640:768]) * SCALE_INDEX, 0.0)
                r_buf[b, part * 64 : part * 64 + 64, cols] = relu
                add = jnp.sum((relu * wcol).reshape(8, 8, BLK), axis=0)
                if part == 0:
                    l_buf[b, :, cols] = add
                else:
                    l_buf[b, :, cols] += add

    def reduce_x(y):
        for b in (2 * y + 1, 2 * y):
            cp = remote(gkb.at[b, :, :, p.c[1]], rc.at[b], cs.at[b], cr.at[b], (0, 0, 0, 1))
            cp.wait()
        for x in range(4):
            b = 2 * y + x % 2
            v1[y, x] = (gkb[b, :, x // 2, p.c[0]] + rc[b, :, x // 2]).astype(BF16)
        own = 2 * y + p.x_low[0]
        v2[y] = gkb[own, :, p.x_high[0], p.c[0]] + rc[own, :, p.x_high[0]]
        for cp in x_copies(y):
            cp.start()

    def x_copies(y):
        return [
            remote(v1.at[y, p.x[j]], rx.at[y, j - 1], xs.at[y, j - 1], xr.at[y, j - 1], (j, 0, 0, 0))
            for j in range(1, 4)
        ]

    def plane_copy(y, j):
        slot = p.y[0] * 4 + p.z[0]
        return pltpu.make_async_remote_copy(
            src_ref=v2.at[y, p.z[j]],
            dst_ref=rv.at[slot],
            send_sem=vs.at[y, j],
            recv_sem=vr.at[slot],
            device_id=dev(y * 8 + p.xl4[0] + p.z[j], p.group),
            device_id_type=MESH,
        )

    def plane_each(y, action):
        for j in range(4):
            if j:
                action(plane_copy(y, j))
            else:

                @pl.when(p.y[0] != y)
                def _():
                    action(plane_copy(y, 0))

    def finish_x(y):
        for cp in x_copies(y):
            cp.wait()
        v2[y] = v2[y] + rx[y, 0].astype(F32) + rx[y, 1].astype(F32) + rx[y, 2].astype(F32)
        plane_each(y, lambda cp: cp.start())

    pltpu.make_async_copy(recv0, recv0, qr.at[0]).wait()
    pltpu.make_async_copy(wrecv0, wrecv0, wr.at[0]).wait()
    forward(0)
    pltpu.make_async_copy(recv1, recv1, qr.at[1]).wait()
    pltpu.make_async_copy(wrecv1, wrecv1, wr.at[1]).wait()
    forward(1)

    gkt[...] = jnp.zeros_like(gkt)
    for b in range(7, -1, -1):
        n = (b + 1) * BLK
        h, g, hl = half_of(b)
        target = dot(fold_t, t_buf[b, :, 0:n], HIGHEST)
        logits = dot(fold_l, l_buf[b, :, 0:n], HIGHEST)
        visible = iota((8, n), 1) - (iota((8, n), 0) // 2) % 2 <= e2 + b * BLK
        logits = jnp.where(visible, logits, NEG)
        top = jnp.max(logits, axis=1, keepdims=True)
        expo = jnp.exp(logits - top)
        probs = expo / jnp.sum(expo, axis=1, keepdims=True)
        token = jnp.broadcast_to(wrecv0[g, 0], (8, 128))
        token = jnp.sum(jnp.where(lane8 == 8 + hl * 2 + row8, token, 0.0), axis=1, keepdims=True)
        l_buf[b, :, 0:n] = token * (probs - target)

        queries = jnp.concatenate([index_queries(part, h) for part in range(2)], axis=0)
        wcol = jnp.concatenate([weight_column(part, g, hl) for part in range(2)], axis=0)
        queries_t = queries.T
        wscaled = wcol * SCALE_INDEX
        gq_sum = jnp.zeros((128, 128), F32)
        gw_sum = jnp.zeros((128, 128), F32)
        for kb in range(b + 1):
            cols = slice(kb * BLK, kb * BLK + BLK)
            relu = r_buf[b, :, cols]
            dl = jnp.broadcast_to(l_buf[b, :, cols][None], (16, 8, BLK)).reshape(128, BLK)
            gwp = dl * relu
            gw_sum = gw_sum + gwp[:, 0:128] + gwp[:, 128:256]
            grad = jnp.where(relu > 0.0, dl * wscaled, 0.0).astype(BF16)
            gq_sum = gq_sum + dot(grad, key_block(kb)[:, 640:768])
            gkt[:, cols] += dot(queries_t, grad)
        gq_block[b] = gq_sum.astype(GQ)
        gws = jnp.sum(gw_sum, axis=1, keepdims=True)
        gw_block[b] = dot(gather, jnp.where(l128 == hl * 4 + v128 % 4, gws, 0.0), HIGHEST)
        gkb[b] = gkt[:, b * BLK : b * BLK + BLK].T.reshape(4, 2, 2, 16, 128)
        remote(gkb.at[b, :, :, p.c[1]], rc.at[b], cs.at[b], cr.at[b], (0, 0, 0, 1)).start()

    for h in range(8):
        gq[h] = gq_block[order_ref[h]].reshape(32, 4, 128)
    for g in range(4):
        total = gw_block[order_ref[2 * g]] + gw_block[order_ref[2 * g + 1]]
        gw[g] = total.reshape(32, 1, 128)
    def returned(o):
        heads, group = p.at(o)
        back = (4 - o[2]) % 4
        slot = (back % 2) * 16 + p.y8[o[1]] // 2 + p.x_low[o[0]] * 2 + back // 2
        remote(gq.at[pl.ds(group * 2, 2), slot], gq_out.at[:, p.flat], bs, br, o).start()
        remote(gw.at[group, slot], gw_recv.at[p.flat], us, ur, o).start()

    pltpu.make_async_copy(gq.at[mine, base], gq_out.at[:, p.flat], br).start()
    pltpu.make_async_copy(gw.at[p.group, base], gw_recv.at[p.flat], ur).start()
    for o in ORDER[0:20]:
        returned(o)
    for y in (3, 2, 1, 0):
        reduce_x(y)
    for o in ORDER[20:70]:
        returned(o)
    for y in (3, 2, 1, 0):
        finish_x(y)
    for o in ORDER[70:127]:
        returned(o)
    pltpu.make_async_copy(gw_recv, gw_recv, ur).wait()
    table = gw_recv[...].reshape(128, 128)
    lines = [[None] * 2 for _ in range(2)]
    for i in range(2):
        choose = one_hot(iota((128, 256), 1) == iota((128, 256), 0) * 2 + i)
        part = lax.dot_general(
            table, choose, (((0,), (0,)), ((), ())), precision=HIGHEST, preferred_element_type=F32
        )
        for hl in range(2):
            at = hl * 4 + i * 2
            lines[hl][i] = part[at : at + 2]
    for hl in range(2):
        gw_out[:, hl * 256 : hl * 256 + 256] = lines[hl][0] + lines[hl][1]
    for y in range(4):
        plane_each(y, lambda cp: cp.wait_send())
    total = v2[p.y[0], p.z[0]]
    for dy in range(4):
        for dz in range(4):
            if dy or dz:
                slot = p.y[dy] * 4 + p.z[dz]
                ref = rv.at[slot]
                pltpu.make_async_copy(ref, ref, vr.at[slot]).wait()
                total = total + rv[slot]
    gk_out[...] = total
    pltpu.make_async_copy(gq_out, gq_out, br).wait()
    sent(63 - EARLY, 1)
    sent(64, 2)
    part = gq_out.at[:, pl.ds(0, 127)]
    pltpu.make_async_copy(part, part, bs).wait()
    for ref, sem in ((wsend, ws), (gw_recv, us)):
        part = ref.at[pl.ds(0, 127)]
        pltpu.make_async_copy(part, part, sem).wait()


GQ = BF16
EARLY = 46
FIRST = 20


def fused(*args):
    any_spec = pl.BlockSpec(memory_space=pl.ANY)
    vmem = pl.BlockSpec(memory_space=pltpu.VMEM)
    sem = pltpu.SemaphoreType.DMA
    return pl.pallas_call(
        fused_kernel,
        in_specs=[pl.BlockSpec(memory_space=pltpu.SMEM)] + [any_spec] * 6,
        out_specs=(any_spec, vmem, vmem),
        out_shape=(
            jax.ShapeDtypeStruct((2, 128, 4, 128), GQ),
            jax.ShapeDtypeStruct((2, 512), F32),
            jax.ShapeDtypeStruct((16, 128), F32),
        ),
        scratch_shapes=[
            pltpu.VMEM((4, 576, 512), BF16),
            pltpu.VMEM((1024, 128), BF16),
            pltpu.VMEM((2, 512), F32),
            pltpu.VMEM((1, 512), F32),
            pltpu.VMEM((16, 576), BF16),
            pltpu.VMEM((16, 128), BF16),
            pltpu.VMEM((512, 768), BF16),
            pltpu.VMEM((2, 128, 8, 640), BF16),
            pltpu.VMEM((128, 1, 128), F32),
            pltpu.VMEM((128, 1, 128), F32),
            pltpu.VMEM((8, 16, 8, 640), BF16),
            pltpu.VMEM((8, 16, 8, 640), BF16),
            pltpu.VMEM((4, 16, 1, 128), F32),
            pltpu.VMEM((4, 16, 1, 128), F32),
            pltpu.VMEM((3, 4, 2, 4, 2, 2, 16, 256), BF16),
            pltpu.VMEM((2, 128, 2048), F32),
            pltpu.VMEM((8, 128, 2048), F32),
            pltpu.VMEM((8, 8, 2048), F32),
            pltpu.VMEM((8, 8, 2048), F32),
            pltpu.VMEM((128, 2048), F32),
            pltpu.VMEM((8, 128, 128), GQ),
            pltpu.VMEM((8, 32, 128), F32),
            pltpu.VMEM((8, 32, 4, 128), GQ),
            pltpu.VMEM((4, 32, 1, 128), F32),
            pltpu.VMEM((8, 4, 2, 2, 16, 128), F32),
            pltpu.VMEM((8, 4, 2, 16, 128), F32),
            pltpu.VMEM((4, 4, 4, 16, 128), BF16),
            pltpu.VMEM((4, 3, 4, 16, 128), BF16),
            pltpu.VMEM((4, 4, 16, 128), F32),
            pltpu.VMEM((16, 16, 128), F32),
            sem((9,)),
            sem((3,)),
            sem((2,)),
            sem,
            sem((2,)),
            sem,
            sem((4, 9)),
            sem((4, 9)),
            sem((3, 4)),
            sem((3, 4)),
            sem((8,)),
            sem((8,)),
            sem((4, 3)),
            sem((4, 3)),
            sem((4, 4)),
            sem((16,)),
            sem,
            sem,
            sem,
            sem,
        ],
        compiler_params=pltpu.CompilerParams(
            has_side_effects=True, collective_id=1, vmem_limit_bytes=56 * 1024 * 1024
        ),
        name="fused",
    )(*args)


def finish_kernel(gq, gw, gk, gq_out, gw_out, gk_out):
    gq_out[...] = gq[...].astype(F32)
    gw_out[...] = gw[...]
    gk_out[...] = gk[...]


def finish(gq, gw, gk):
    return pl.pallas_call(
        finish_kernel,
        grid=(2,),
        in_specs=[
            pl.BlockSpec((512, 128), lambda t: (t, 0)),
            pl.BlockSpec((2, 512), lambda t: (0, 0)),
            pl.BlockSpec((16, 128), lambda t: (0, 0)),
        ],
        out_specs=(
            pl.BlockSpec((512, 128), lambda t: (t, 0)),
            pl.BlockSpec((2, 512), lambda t: (0, 0)),
            pl.BlockSpec((16, 128), lambda t: (0, 0)),
        ),
        out_shape=(
            jax.ShapeDtypeStruct((1024, 128), F32),
            jax.ShapeDtypeStruct((2, 512), F32),
            jax.ShapeDtypeStruct((16, 128), F32),
        ),
        name="finish",
    )(gq, gw, gk)


def on_device(q_main, latent, q_index, head_weight, k_index, token_weight, block_order):
    gq, gw, gk = fused(
        block_order,
        jnp.transpose(q_main, (1, 2, 0)),
        q_index.reshape(1024, 128),
        head_weight,
        token_weight.reshape(1, 512),
        latent,
        k_index,
    )
    gq, gw, gk = finish(gq.reshape(1024, 128), gw, gk)
    return gq.reshape(512, 2, 128), gw, gk


def solution(mesh):
    return jax.shard_map(
        on_device,
        mesh=mesh,
        in_specs=(
            P("qgrp", "heads", None),
            P(("heads", "qgrp"), None),
            P("qgrp", "heads", None),
            P("heads", "qgrp"),
            P(("heads", "qgrp"), None),
            P("qgrp"),
            P(),
        ),
        out_specs=(P("qgrp", "heads", None), P("heads", "qgrp"), P(("heads", "qgrp"), None)),
        check_vma=False,
    )
```

```python
import math
import random

import jax
import jax.numpy as jnp
from jax import lax
from jax.experimental import pallas as pl
from jax.experimental.pallas import tpu as pltpu
from jax.sharding import PartitionSpec as P

MESH = pl.DeviceIdType.MESH
SCALE_INDEX = 128.0 ** (-0.5)
EXP_SCALE = 192.0 ** (-0.5) * math.log2(math.e)
NEG = -3.0e38
BLK = 256
F32 = jnp.float32
BF16 = jnp.bfloat16
HIGHEST = lax.Precision.HIGHEST


def far_first():
    every = [(a, b, c, d) for a in range(4) for b in range(4) for c in range(4) for d in range(2)][1:]
    random.Random(1).shuffle(every)
    return sorted(every, key=lambda o: sum(min(v, 4 - v) for v in o[:3]) + o[3] * 0.5)[::-1]


ORDER = far_first()
KEY_CUTS = (0, 16, 40, 80, 127)


class Place:
    def __init__(self):
        h = lax.axis_index("heads")
        q = lax.axis_index("qgrp")
        self.y = [lax.rem(lax.div(h, 8) + k, 4) for k in range(4)]
        self.z = [lax.rem(lax.rem(h, 4) + k, 4) for k in range(4)]
        x = lax.div(q, 2) * 2 + lax.rem(lax.div(h, 4), 2)
        self.x = [lax.rem(x + k, 4) for k in range(4)]
        self.c = [lax.rem(q, 2), 1 - lax.rem(q, 2)]
        self.x_low = [lax.rem(v, 2) for v in self.x]
        self.x_high = [lax.div(v, 2) for v in self.x]
        self.y8 = [v * 8 for v in self.y]
        self.xl4 = [v * 4 for v in self.x_low]
        self.xh2 = [v * 2 for v in self.x_high]
        self.heads, self.group = self.at((0, 0, 0, 0))
        self.flat = self.heads * 4 + self.group

    def at(self, o):
        dx, dy, dz, dc = o
        return self.y8[dy] + self.xl4[dx] + self.z[dz], self.xh2[dx] + self.c[dc]


def dev(heads, group):
    return {"heads": heads, "qgrp": group}


def enter(place):
    sem = pltpu.get_barrier_semaphore()
    for o in ORDER:
        pl.semaphore_signal(sem, inc=1, device_id=dev(*place.at(o)), device_id_type=MESH)
    return sem


def iota(shape, dim):
    return lax.broadcasted_iota(jnp.int32, shape, dim)


def dot_t(a, b, precision=None):
    return lax.dot_general(
        a, b, (((1,), (1,)), ((), ())), precision=precision, preferred_element_type=F32
    )


def dot(a, b, precision=None):
    return jnp.dot(a, b, precision=precision, preferred_element_type=F32)


def one_hot(mask):
    return jnp.where(mask, 1.0, 0.0)


PARTS = ((0, 2), (1, 3))


def fused_kernel(
    order_ref,
    main_hbm,
    index_hbm,
    weight_hbm,
    token_hbm,
    latent_hbm,
    key_hbm,
    gq_out,
    gw_out,
    gk_out,
    main,
    index,
    weight,
    token_in,
    latent,
    key,
    perm,
    packed,
    wsend,
    gw_recv,
    recv0,
    recv1,
    wrecv0,
    wrecv1,
    keys,
    s_buf,
    r_buf,
    t_buf,
    l_buf,
    gkt,
    gq_block,
    gw_block,
    gq,
    gw,
    gkb,
    rc,
    v1,
    rx,
    v2,
    rv,
    ms,
    qs,
    qr,
    ws,
    wr,
    ls,
    ags,
    agr,
    fs,
    fr,
    cs,
    cr,
    xs,
    xr,
    vs,
    vr,
    bs,
    br,
    us,
    ur,
):
    p = Place()
    tiles = [
        pltpu.make_async_copy(
            main_hbm.at[:, :, pl.ds(t * 128, 128)], main.at[:, :, pl.ds(t * 128, 128)], ms.at[t]
        )
        for t in range(4)
    ]
    small = [
        pltpu.make_async_copy(src, dst, ms.at[4 + at])
        for at, (src, dst) in enumerate(
            (
                (latent_hbm, latent),
                (key_hbm, key),
                (index_hbm, index),
                (weight_hbm, weight),
                (token_hbm, token_in),
            )
        )
    ]
    for cp in small[0:2] + tiles + small[2:]:
        cp.start()
    barrier = enter(p)
    recv = (recv0, recv1)
    wrecv = (wrecv0, wrecv1)
    mine = pl.ds(p.group * 2, 2)
    base = p.y[0] * 4 + p.x_low[0] * 2

    def remote(src, dst, ssem, rsem, o):
        return pltpu.make_async_remote_copy(
            src_ref=src,
            dst_ref=dst,
            send_sem=ssem,
            recv_sem=rsem,
            device_id=dev(*p.at(o)),
            device_id_type=MESH,
        )

    def key_phase(number):
        copies = []
        for color, axes in enumerate(("zyx", "yxz", "xzy")):
            done = axes[:number]
            ref = keys.at[
                color,
                slice(None) if "y" in done else p.y[0],
                slice(None) if "x" in done else p.x_low[0],
                slice(None) if "z" in done else p.z[0],
                slice(None) if "x" in done else p.x_high[0],
                p.c[0],
            ]
            for j in range(1, 4):
                o = tuple(j if axis == axes[number] else 0 for axis in "xyz") + (0,)
                at = color * 3 + j - 1
                copies.append(remote(ref, ref, ags.at[number, at], agr.at[number, at], o))
        return copies

    def to_partner(number, at, ref):
        return remote(ref, ref, fs.at[number, at], fr.at[number, at], (0, 0, 0, 1))

    def block(color, axes, number, o):
        done = axes[:number]
        return keys.at[
            color,
            slice(None) if "y" in done else p.y[-o[1] % 4],
            slice(None) if "x" in done else p.x_low[-o[0] % 4],
            slice(None) if "z" in done else p.z[-o[2] % 4],
            slice(None) if "x" in done else p.x_high[-o[0] % 4],
            p.c[0],
        ]

    def sent(count, at):
        part = packed.at[:, pl.ds(0, count)]
        pltpu.make_async_copy(part, part, qs.at[at]).wait()

    def send(o, at):
        heads, group = p.at(o)
        e = heads * 4 + group
        part, slot = o[2] % 2, o[2] // 2
        remote(packed.at[:, e], recv[part].at[mine, base + slot], qs.at[at], qr.at[part], o).start()
        remote(wsend.at[e], wrecv[part].at[p.group, base + slot], ws, wr.at[part], o).start()

    def pack_tile(t):
        lanes = pl.ds(t * 128, 128)
        both = jnp.concatenate([main[h, :, lanes] for h in range(4)], axis=1)
        rows = dot_t(perm[:, 0:512], both)
        tail = dot(perm[:, 512:768], index[t * 256 : t * 256 + 256])
        lane, row = iota((512, 128), 1), iota((512, 128), 0)
        tail = jnp.where(row % 2 == 0, pltpu.roll(tail, 64, 1), tail)
        last = jnp.concatenate([rows[:, 512:576], jnp.zeros((512, 64), F32)], axis=1)
        last = jnp.where(lane < 64, last, tail)
        full = jnp.concatenate([rows[:, 0:512], last], axis=1).astype(BF16)
        packed[t // 2, (t % 2) * 64 : (t % 2) * 64 + 64] = full.reshape(64, 8, 640)

    def pack_weights():
        total = jnp.zeros((128, 128), F32)
        sub = iota((128, 256), 0)
        for hl in range(2):
            cols = slice(hl * 256, hl * 256 + 256)
            for i in range(2):
                table = jnp.zeros((128, 256), F32)
                for at, line in (
                    (hl * 4 + i * 2, weight[0:1, cols]),
                    (hl * 4 + i * 2 + 1, weight[1:2, cols]),
                    (8 + hl * 2 + i, token_in[0:1, cols]),
                ):
                    table = jnp.where(sub == at, jnp.broadcast_to(line, (128, 256)), table)
                choose = one_hot(iota((128, 256), 1) == iota((128, 256), 0) * 2 + i)
                total = total + dot_t(choose, table, HIGHEST)
        wsend[...] = total.reshape(128, 1, 128)

    small[0].wait()
    small[1].wait()
    at = (p.y[0], p.x_low[0], p.z[0], p.x_high[0], p.c[0])
    keys[(0,) + at] = latent[:, 0:256]
    keys[(1,) + at] = latent[:, 256:512]
    keys[(2,) + at] = jnp.concatenate([latent[:, 512:576], jnp.zeros((16, 64), BF16), key[...]], axis=1)
    out, src = iota((512, 512), 0), iota((512, 512), 1)
    perm[:, 0:512] = one_hot(out == (src % 128) * 4 + src // 128).astype(BF16)
    out, src = iota((512, 256), 0), iota((512, 256), 1)
    perm[:, 512:768] = one_hot(src == out // 2).astype(BF16)
    pl.semaphore_wait(barrier, 127)
    order = [o for part in PARTS for o in ORDER if o[2] in part]
    colors = list(enumerate(("zyx", "yxz", "xzy")))
    forwards = []
    for number in range(3):
        phase = key_phase(number)
        for cp in phase:
            cp.start()
        if number == 0:
            for cp in small[2:]:
                cp.wait()
            pack_weights()
            for t in range(2):
                tiles[t].wait()
                pack_tile(t)
        elif number == 1:
            for t in range(2, 4):
                tiles[t].wait()
                pack_tile(t)
            pltpu.make_async_copy(packed.at[:, p.flat], recv0.at[mine, base], qr.at[0]).start()
            pltpu.make_async_copy(wsend.at[p.flat], wrecv0.at[p.group, base], wr.at[0]).start()
            for at, o in enumerate(order[0:FIRST]):
                send(o, at // EARLY)
        else:
            for color, axes in colors:
                cp = to_partner(color, 0, block(color, axes, 2, (0, 0, 0, 0)))
                cp.start()
                forwards.append(cp)
            for at, o in enumerate(order[FIRST:63], FIRST):
                send(o, at // EARLY)
            sent(EARLY, 0)
            for o in order[63:127]:
                send(o, 2)
        for j in range(1, 4):
            for color, axes in colors:
                phase[color * 3 + j - 1].wait()
                if number == 2:
                    o = tuple(j if axis == axes[2] else 0 for axis in "xyz")
                    cp = to_partner(color, j, block(color, axes, 2, o))
                    cp.start()
                    forwards.append(cp)
    for cp in forwards:
        cp.wait()

    e2 = p.flat * 2
    spread = one_hot(iota((64, 16), 1) == iota((64, 16), 0) // 4)
    gather = one_hot(iota((32, 128), 1) // 4 == iota((32, 128), 0))
    even = one_hot(iota((64, 128), 1) == iota((64, 128), 0) * 2).astype(BF16)
    odd = one_hot(iota((64, 128), 1) == iota((64, 128), 0) * 2 + 1).astype(BF16)
    f_out, f_in = iota((8, 8), 0), iota((8, 8), 1)
    fold_t = one_hot(f_in // 4 == (f_out // 2) % 2)
    fold_l = one_hot((f_in // 2) % 2 == (f_out // 2) % 2)
    l64, v64 = iota((64, 128), 1), iota((64, 128), 0)
    l128, v128 = iota((128, 128), 1), iota((128, 128), 0)
    row8, lane8 = (iota((8, 128), 0) // 2) % 2, iota((8, 128), 1)

    def half_of(b):
        h = 0
        for at in range(1, 8):
            h = jnp.where(order_ref[at] == b, at, h)
        return h, lax.div(h, 2), lax.rem(h, 2)

    def index_queries(part, h):
        tail = recv[part][h, :, :, 512:640].reshape(128, 128)
        low = pltpu.roll(dot(even, tail), 64, 1)
        return jnp.where(l64 < 64, low, dot(odd, tail)).astype(BF16)

    def weight_column(part, g, hl):
        table = dot(spread, wrecv[part][g, :, 0, :], HIGHEST)
        return jnp.sum(jnp.where(l64 == hl * 4 + v64 % 4, table, 0.0), axis=1, keepdims=True)

    def key_block(kb):
        parts = [keys[color, kb // 2, kb % 2].reshape(256, 256) for color in range(3)]
        return jnp.concatenate(parts, axis=1)

    def forward(part):
        for b in range(7, -1, -1):
            n = (b + 1) * BLK
            par = b % 2
            h, g, hl = half_of(b)
            x = recv[part][h].reshape(128, 640)
            for kb in range(b + 1):
                cols = slice(kb * BLK, kb * BLK + BLK)
                s = dot_t(x, key_block(kb)[:, 0:640])
                if kb == b:
                    row = (iota((128, BLK), 0) % 8) // 4
                    s = jnp.where(iota((128, BLK), 1) - row <= e2, s, NEG)
                s_buf[par, :, cols] = s

            def softmax_rows(r):
                rows = slice(r * 32, r * 32 + 32)
                s = s_buf[par, rows, 0:n]
                top = jnp.max(s, axis=1, keepdims=True)
                w = jnp.exp2((s - top) * EXP_SCALE)
                inv = (1.0 / 128.0) / jnp.sum(w, axis=1, keepdims=True)
                add = jnp.sum((w * inv).reshape(4, 8, n), axis=0)
                if part == 0 and r == 0:
                    t_buf[b, :, 0:n] = add
                else:
                    t_buf[b, :, 0:n] += add

            for r in range(4):
                softmax_rows(r)

            queries = index_queries(part, h)
            wcol = weight_column(part, g, hl)
            for kb in range(b + 1):
                cols = slice(kb * BLK, kb * BLK + BLK)
                relu = jnp.maximum(dot_t(queries, key_block(kb)[:, 640:768]) * SCALE_INDEX, 0.0)
                r_buf[b, part * 64 : part * 64 + 64, cols] = relu
                add = jnp.sum((relu * wcol).reshape(8, 8, BLK), axis=0)
                if part == 0:
                    l_buf[b, :, cols] = add
                else:
                    l_buf[b, :, cols] += add

    def reduce_x(y):
        for b in (2 * y + 1, 2 * y):
            cp = remote(gkb.at[b, :, :, p.c[1]], rc.at[b], cs.at[b], cr.at[b], (0, 0, 0, 1))
            cp.wait()
        for x in range(4):
            b = 2 * y + x % 2
            v1[y, x] = (gkb[b, :, x // 2, p.c[0]] + rc[b, :, x // 2]).astype(BF16)
        own = 2 * y + p.x_low[0]
        v2[y] = gkb[own, :, p.x_high[0], p.c[0]] + rc[own, :, p.x_high[0]]
        for cp in x_copies(y):
            cp.start()

    def x_copies(y):
        return [
            remote(v1.at[y, p.x[j]], rx.at[y, j - 1], xs.at[y, j - 1], xr.at[y, j - 1], (j, 0, 0, 0))
            for j in range(1, 4)
        ]

    def plane_copy(y, j):
        slot = p.y[0] * 4 + p.z[0]
        return pltpu.make_async_remote_copy(
            src_ref=v2.at[y, p.z[j]],
            dst_ref=rv.at[slot],
            send_sem=vs.at[y, j],
            recv_sem=vr.at[slot],
            device_id=dev(y * 8 + p.xl4[0] + p.z[j], p.group),
            device_id_type=MESH,
        )

    def plane_each(y, action):
        for j in range(4):
            if j:
                action(plane_copy(y, j))
            else:

                @pl.when(p.y[0] != y)
                def _():
                    action(plane_copy(y, 0))

    def finish_x(y):
        for cp in x_copies(y):
            cp.wait()
        v2[y] = v2[y] + rx[y, 0].astype(F32) + rx[y, 1].astype(F32) + rx[y, 2].astype(F32)
        plane_each(y, lambda cp: cp.start())

    pltpu.make_async_copy(recv0, recv0, qr.at[0]).wait()
    pltpu.make_async_copy(wrecv0, wrecv0, wr.at[0]).wait()
    forward(0)
    pltpu.make_async_copy(recv1, recv1, qr.at[1]).wait()
    pltpu.make_async_copy(wrecv1, wrecv1, wr.at[1]).wait()
    forward(1)

    gkt[...] = jnp.zeros_like(gkt)
    for b in range(7, -1, -1):
        n = (b + 1) * BLK
        h, g, hl = half_of(b)
        target = dot(fold_t, t_buf[b, :, 0:n], HIGHEST)
        logits = dot(fold_l, l_buf[b, :, 0:n], HIGHEST)
        visible = iota((8, n), 1) - (iota((8, n), 0) // 2) % 2 <= e2 + b * BLK
        logits = jnp.where(visible, logits, NEG)
        top = jnp.max(logits, axis=1, keepdims=True)
        expo = jnp.exp(logits - top)
        probs = expo / jnp.sum(expo, axis=1, keepdims=True)
        token = jnp.broadcast_to(wrecv0[g, 0], (8, 128))
        token = jnp.sum(jnp.where(lane8 == 8 + hl * 2 + row8, token, 0.0), axis=1, keepdims=True)
        l_buf[b, :, 0:n] = token * (probs - target)

        queries = jnp.concatenate([index_queries(part, h) for part in range(2)], axis=0)
        wcol = jnp.concatenate([weight_column(part, g, hl) for part in range(2)], axis=0)
        queries_t = queries.T
        wscaled = wcol * SCALE_INDEX
        gq_sum = jnp.zeros((128, 128), F32)
        gw_sum = jnp.zeros((128, 128), F32)
        for kb in range(b + 1):
            cols = slice(kb * BLK, kb * BLK + BLK)
            relu = r_buf[b, :, cols]
            dl = jnp.broadcast_to(l_buf[b, :, cols][None], (16, 8, BLK)).reshape(128, BLK)
            gwp = dl * relu
            gw_sum = gw_sum + gwp[:, 0:128] + gwp[:, 128:256]
            grad = jnp.where(relu > 0.0, dl * wscaled, 0.0).astype(BF16)
            gq_sum = gq_sum + dot(grad, key_block(kb)[:, 640:768])
            gkt[:, cols] += dot(queries_t, grad)
        gq_block[b] = gq_sum.astype(GQ)
        gws = jnp.sum(gw_sum, axis=1, keepdims=True)
        gw_block[b] = dot(gather, jnp.where(l128 == hl * 4 + v128 % 4, gws, 0.0), HIGHEST)
        gkb[b] = gkt[:, b * BLK : b * BLK + BLK].T.reshape(4, 2, 2, 16, 128)
        remote(gkb.at[b, :, :, p.c[1]], rc.at[b], cs.at[b], cr.at[b], (0, 0, 0, 1)).start()

    def returned(o):
        heads, group = p.at(o)
        back = (4 - o[2]) % 4
        slot = (back % 2) * 16 + p.y8[o[1]] // 2 + p.x_low[o[0]] * 2 + back // 2
        remote(gq.at[pl.ds(group * 2, 2), slot], gq_out.at[:, p.flat], bs, br, o).start()
        remote(gw.at[group, slot], gw_recv.at[p.flat], us, ur, o).start()

    for y in (3, 2, 1, 0):
        reduce_x(y)
    for h in range(8):
        gq[h] = gq_block[order_ref[h]].reshape(32, 4, 128)
    for g in range(4):
        total = gw_block[order_ref[2 * g]] + gw_block[order_ref[2 * g + 1]]
        gw[g] = total.reshape(32, 1, 128)
    pltpu.make_async_copy(gq.at[mine, base], gq_out.at[:, p.flat], br).start()
    pltpu.make_async_copy(gw.at[p.group, base], gw_recv.at[p.flat], ur).start()
    for o in ORDER[0:40]:
        returned(o)
    for y in (3, 2, 1, 0):
        finish_x(y)
    for o in ORDER[40:127]:
        returned(o)
    pltpu.make_async_copy(gw_recv, gw_recv, ur).wait()
    table = gw_recv[...].reshape(128, 128)
    lines = [[None] * 2 for _ in range(2)]
    for i in range(2):
        choose = one_hot(iota((128, 256), 1) == iota((128, 256), 0) * 2 + i)
        part = lax.dot_general(
            table, choose, (((0,), (0,)), ((), ())), precision=HIGHEST, preferred_element_type=F32
        )
        for hl in range(2):
            at = hl * 4 + i * 2
            lines[hl][i] = part[at : at + 2]
    for hl in range(2):
        gw_out[:, hl * 256 : hl * 256 + 256] = lines[hl][0] + lines[hl][1]
    for y in range(4):
        plane_each(y, lambda cp: cp.wait_send())
    total = v2[p.y[0], p.z[0]]
    for dy in range(4):
        for dz in range(4):
            if dy or dz:
                slot = p.y[dy] * 4 + p.z[dz]
                ref = rv.at[slot]
                pltpu.make_async_copy(ref, ref, vr.at[slot]).wait()
                total = total + rv[slot]
    gk_out[...] = total
    pltpu.make_async_copy(gq_out, gq_out, br).wait()
    sent(63 - EARLY, 1)
    sent(64, 2)
    part = gq_out.at[:, pl.ds(0, 127)]
    pltpu.make_async_copy(part, part, bs).wait()
    for ref, sem in ((wsend, ws), (gw_recv, us)):
        part = ref.at[pl.ds(0, 127)]
        pltpu.make_async_copy(part, part, sem).wait()


GQ = BF16
EARLY = 46
FIRST = 20


def fused(*args):
    any_spec = pl.BlockSpec(memory_space=pl.ANY)
    vmem = pl.BlockSpec(memory_space=pltpu.VMEM)
    sem = pltpu.SemaphoreType.DMA
    return pl.pallas_call(
        fused_kernel,
        in_specs=[pl.BlockSpec(memory_space=pltpu.SMEM)] + [any_spec] * 6,
        out_specs=(any_spec, vmem, vmem),
        out_shape=(
            jax.ShapeDtypeStruct((2, 128, 4, 128), GQ),
            jax.ShapeDtypeStruct((2, 512), F32),
            jax.ShapeDtypeStruct((16, 128), F32),
        ),
        scratch_shapes=[
            pltpu.VMEM((4, 576, 512), BF16),
            pltpu.VMEM((1024, 128), BF16),
            pltpu.VMEM((2, 512), F32),
            pltpu.VMEM((1, 512), F32),
            pltpu.VMEM((16, 576), BF16),
            pltpu.VMEM((16, 128), BF16),
            pltpu.VMEM((512, 768), BF16),
            pltpu.VMEM((2, 128, 8, 640), BF16),
            pltpu.VMEM((128, 1, 128), F32),
            pltpu.VMEM((128, 1, 128), F32),
            pltpu.VMEM((8, 16, 8, 640), BF16),
            pltpu.VMEM((8, 16, 8, 640), BF16),
            pltpu.VMEM((4, 16, 1, 128), F32),
            pltpu.VMEM((4, 16, 1, 128), F32),
            pltpu.VMEM((3, 4, 2, 4, 2, 2, 16, 256), BF16),
            pltpu.VMEM((2, 128, 2048), F32),
            pltpu.VMEM((8, 128, 2048), F32),
            pltpu.VMEM((8, 8, 2048), F32),
            pltpu.VMEM((8, 8, 2048), F32),
            pltpu.VMEM((128, 2048), F32),
            pltpu.VMEM((8, 128, 128), GQ),
            pltpu.VMEM((8, 32, 128), F32),
            pltpu.VMEM((8, 32, 4, 128), GQ),
            pltpu.VMEM((4, 32, 1, 128), F32),
            pltpu.VMEM((8, 4, 2, 2, 16, 128), F32),
            pltpu.VMEM((8, 4, 2, 16, 128), F32),
            pltpu.VMEM((4, 4, 4, 16, 128), BF16),
            pltpu.VMEM((4, 3, 4, 16, 128), BF16),
            pltpu.VMEM((4, 4, 16, 128), F32),
            pltpu.VMEM((16, 16, 128), F32),
            sem((9,)),
            sem((3,)),
            sem((2,)),
            sem,
            sem((2,)),
            sem,
            sem((4, 9)),
            sem((4, 9)),
            sem((3, 4)),
            sem((3, 4)),
            sem((8,)),
            sem((8,)),
            sem((4, 3)),
            sem((4, 3)),
            sem((4, 4)),
            sem((16,)),
            sem,
            sem,
            sem,
            sem,
        ],
        compiler_params=pltpu.CompilerParams(
            has_side_effects=True, collective_id=1, vmem_limit_bytes=56 * 1024 * 1024
        ),
        name="fused",
    )(*args)


def finish_kernel(gq, gw, gk, gq_out, gw_out, gk_out):
    gq_out[...] = gq[...].astype(F32)
    gw_out[...] = gw[...]
    gk_out[...] = gk[...]


def finish(gq, gw, gk):
    return pl.pallas_call(
        finish_kernel,
        grid=(2,),
        in_specs=[
            pl.BlockSpec((512, 128), lambda t: (t, 0)),
            pl.BlockSpec((2, 512), lambda t: (0, 0)),
            pl.BlockSpec((16, 128), lambda t: (0, 0)),
        ],
        out_specs=(
            pl.BlockSpec((512, 128), lambda t: (t, 0)),
            pl.BlockSpec((2, 512), lambda t: (0, 0)),
            pl.BlockSpec((16, 128), lambda t: (0, 0)),
        ),
        out_shape=(
            jax.ShapeDtypeStruct((1024, 128), F32),
            jax.ShapeDtypeStruct((2, 512), F32),
            jax.ShapeDtypeStruct((16, 128), F32),
        ),
        name="finish",
    )(gq, gw, gk)


def on_device(q_main, latent, q_index, head_weight, k_index, token_weight, block_order):
    gq, gw, gk = fused(
        block_order,
        jnp.transpose(q_main, (1, 2, 0)),
        q_index.reshape(1024, 128),
        head_weight,
        token_weight.reshape(1, 512),
        latent,
        k_index,
    )
    gq, gw, gk = finish(gq.reshape(1024, 128), gw, gk)
    return gq.reshape(512, 2, 128), gw, gk


def solution(mesh):
    return jax.shard_map(
        on_device,
        mesh=mesh,
        in_specs=(
            P("qgrp", "heads", None),
            P(("heads", "qgrp"), None),
            P("qgrp", "heads", None),
            P("heads", "qgrp"),
            P(("heads", "qgrp"), None),
            P("qgrp"),
            P(),
        ),
        out_specs=(P("qgrp", "heads", None), P("heads", "qgrp"), P(("heads", "qgrp"), None)),
        check_vma=False,
    )
```
